256 devices in a mesh: img: 4 (over y), seq: 64 (over z, x, core).
Axes of the slice: x: 4, y: 4, z: 8, core: 2. Of those that a mesh axis runs over, the one named last changes fastest.
Arguments:
- query_proj: bfloat16 [4, 8192, 1280], P('img', 'seq'), may hold values from -6 to 6
- key_proj: bfloat16 [4, 8192, 1280], P('img', 'seq'), may hold values from -6 to 6
- value_proj: bfloat16 [4, 8192, 1280], P('img', 'seq'), may hold values from -12 to 12
- merge_cells: int32 [4, 2048, 4], P('img', 'seq'), may hold values from 0 to 8191, as said below
- unmerge: int32 [4, 8192], P('img', 'seq'), may hold values from 0 to 2047, as said below
- grad_out: bfloat16 [4, 8192, 1280], P('img', 'seq'), may hold values from -9 to 9
- query_gain: float32 [64], replicated, may hold values from 1 to 2.5
- key_gain: float32 [64], replicated, may hold values from 1 to 2.5
Outputs:
- attended: bfloat16 [4, 8192, 1280], P('img', 'seq')
- grad_query: bfloat16 [4, 8192, 1280], P('img', 'seq')
- grad_key: bfloat16 [4, 8192, 1280], P('img', 'seq')
- grad_value: bfloat16 [4, 8192, 1280], P('img', 'seq')
- grad_query_gain: float32 [64], replicated
- grad_key_gain: float32 [64], replicated
The draws below stay inside these ranges and needn't reach their ends.
Inputs may be any that keep to these rules, and one draw needn't show every extreme that they name: `merge_cells`: row c of an image lists, in some order, the four tokens of one 2x2 cell: columns j and j + 1 (modulo 64) of image rows 2 i and 2 i + 1, where token r * 64 + s stands at row r and column s and j has one parity within each pair of rows; every token lies in exactly one cell; cell c and its four tokens are held by the same seq index. `unmerge`: entry t is the row of merge_cells of the same image that lists token t.
All inputs are finite; a program needn't handle non-finite values.
Results may differ from the reference program's by a relative error of at most 0.012.
Values may be sent and summed in bfloat16 or wider, within the bound.
A program may use at most 128 MiB of HBM per device.

```python
import math
import jax
import jax.numpy as jnp
from jax import lax

HD = 64
H = 20
COLS = 64
HE = 1280
TOK_DEV = 128
TOKENS = 8192
C_DEV = 32
CELLS = 2048
IMAGES = 4


def cell_layout(key):
    pair_count = TOKENS // (2 * COLS)
    half_cols = COLS // 2
    devices = TOKENS // TOK_DEV
    col_phase = jax.random.randint(jax.random.fold_in(key, 3), (pair_count, 1), 0, 2)
    pair_ids = jnp.arange(pair_count, dtype=jnp.int32)[:, None]
    col_slot = jnp.arange(half_cols, dtype=jnp.int32)[None, :]
    left_col = (2 * col_slot + col_phase) % COLS
    right_col = (2 * col_slot + 1 + col_phase) % COLS
    top_token = 2 * pair_ids * COLS
    cell_tokens = jnp.stack([top_token + left_col, top_token + right_col, top_token + COLS + left_col, top_token + COLS + right_col], axis=-1).reshape(CELLS, 4)
    rotation = jax.random.randint(jax.random.fold_in(key, 4), (CELLS, 1), 0, 4)
    entry_order = (jnp.arange(4, dtype=jnp.int32)[None, :] + rotation) % 4
    cell_tokens = jnp.take_along_axis(cell_tokens, entry_order, axis=1)
    sub_keys = jax.random.split(jax.random.fold_in(key, 5), devices)
    permuted = jax.vmap(lambda sub_key: jax.random.permutation(sub_key, C_DEV))(sub_keys)
    cell_slots = (permuted.astype(jnp.int32) + (jnp.arange(devices, dtype=jnp.int32) * C_DEV)[:, None]).reshape(CELLS)
    merge_table = jnp.zeros((CELLS, 4), jnp.int32).at[cell_slots].set(cell_tokens)
    unmerge_table = jnp.zeros((TOKENS,), jnp.int32).at[cell_tokens.reshape(-1)].set(jnp.repeat(cell_slots, 4))
    return (merge_table, unmerge_table)


def draw_merge_cells(key, part):
    base = jax.random.fold_in(key, 7)
    return jax.vmap(lambda image_index: cell_layout(jax.random.fold_in(base, image_index))[0])(jnp.arange(IMAGES, dtype=jnp.int32))


def draw_unmerge(key, part):
    base = jax.random.fold_in(key, 7)
    return jax.vmap(lambda image_index: cell_layout(jax.random.fold_in(base, image_index))[1])(jnp.arange(IMAGES, dtype=jnp.int32))


def draw_grad_out(key, part):
    noise_vals = jax.random.normal(jax.random.fold_in(key, 11), (IMAGES, TOKENS, HE), jnp.float32)
    position = (jnp.arange(IMAGES, dtype=jnp.float32)[:, None] * TOKENS + jnp.arange(TOKENS, dtype=jnp.float32)[None, :]) / (IMAGES * TOKENS - 1)
    row_scale = 0.5 + position
    return (jnp.clip(noise_vals, -4.0, 4.0) * row_scale[:, :, None]).astype(jnp.bfloat16)


def levels(rng, dims, shards, low, largest):
    def one(axis_at, blocks):
        heights = jax.random.uniform(jax.random.fold_in(jax.random.fold_in(rng, 6), axis_at), (blocks,), jnp.float32, low / len(shards), largest / len(shards))
        return jnp.repeat(jnp.exp(heights), dims[axis_at] // blocks).reshape((-1,) + (1,) * (len(dims) - axis_at - 1))

    gain = one(*shards[0])
    for cut in shards[1:]:
        gain = gain * one(*cut)
    return gain


def bell_draw(stream_key, dims, scale, bound, cuts=(), kind=jnp.bfloat16):
    values = scale * jax.random.normal(stream_key, dims, jnp.float32)
    if cuts:
        values = values * levels(stream_key, dims, cuts, -0.22, 0.18)
    return jnp.clip(values, -bound, bound).astype(kind)


def setup_inputs(seed: int = 0) -> dict:
    streams_of = jax.random.split(jax.random.key(seed), 9)
    return {
        "query_proj": bell_draw(streams_of[0], (IMAGES, TOKENS, HE), 1.0, 6.0, ((0, 4), (1, 64))),
        "key_proj": bell_draw(streams_of[1], (IMAGES, TOKENS, HE), 1.0, 6.0, ((0, 4), (1, 64))),
        "value_proj": bell_draw(streams_of[2], (IMAGES, TOKENS, HE), 2.0, 12.0, ((0, 4), (1, 64))),
        "merge_cells": draw_merge_cells(jax.random.fold_in(streams_of[8], 71), 0),
        "unmerge": draw_unmerge(jax.random.fold_in(streams_of[8], 71), 0),
        "grad_out": draw_grad_out(jax.random.fold_in(streams_of[8], 71), 0),
        "query_gain": jnp.clip(jnp.exp(jax.random.uniform(streams_of[6], (HD,), jnp.float32, math.log(1.0), math.log(2.5))), 1.0, 2.5),
        "key_gain": jnp.clip(jnp.exp(jax.random.uniform(streams_of[7], (HD,), jnp.float32, math.log(1.0), math.log(2.5))), 1.0, 2.5),
    }


EPSILON = 1e-06

def normalize(inputs, gain_row):
    row_scale = lax.rsqrt(lax.optimization_barrier(jnp.mean(inputs * inputs, axis=-1, keepdims=True)) + EPSILON)
    unit_vals = inputs * row_scale
    return (unit_vals, row_scale, unit_vals * gain_row)

def norm_back(grad_normed, unit_vals, row_scale, gain_row):
    grad_unit = grad_normed * gain_row
    mean_inner = lax.optimization_barrier(jnp.mean(grad_unit * unit_vals, axis=-1, keepdims=True))
    return row_scale * (grad_unit - unit_vals * mean_inner)

def head_pass(pieces):
    queries, key_rows, value_rows, upstream = pieces
    scores = jnp.dot(queries, key_rows.T, preferred_element_type=jnp.float32) * 0.125
    exp_scores = jnp.exp(scores)
    row_total = lax.optimization_barrier(jnp.sum(exp_scores, axis=1, keepdims=True))
    attended = (jnp.dot(exp_scores.astype(jnp.bfloat16), value_rows, preferred_element_type=jnp.float32) / row_total).astype(jnp.bfloat16)
    attention = exp_scores / row_total
    grad_values = jnp.dot(attention.astype(jnp.bfloat16).T, upstream, preferred_element_type=jnp.float32)
    grad_weights = jnp.dot(upstream, value_rows.T, preferred_element_type=jnp.float32)
    row_inner = lax.optimization_barrier(jnp.sum(upstream.astype(jnp.float32) * attended.astype(jnp.float32), axis=1, keepdims=True))
    grad_scores = (attention * (grad_weights - row_inner)).astype(jnp.bfloat16)
    grad_queries = jnp.dot(grad_scores, key_rows, preferred_element_type=jnp.float32) * 0.125
    grad_keys = jnp.dot(grad_scores.T, queries, preferred_element_type=jnp.float32) * 0.125
    return (attended, grad_queries, grad_keys, grad_values)

def by_head(array, row_count):
    return array.reshape(row_count, H, HD).transpose(1, 0, 2)

def one_image(pieces, query_gain, key_gain):
    query_proj, key_proj, value_proj, merge_cells, unmerge, grad_out = pieces
    q_unit, q_scale, q_normed = normalize(query_proj.astype(jnp.float32).reshape(TOKENS, H, HD), query_gain)
    q_bf = q_normed.astype(jnp.bfloat16)
    k_unit, k_scale, k_normed = normalize(key_proj.astype(jnp.float32).reshape(TOKENS, H, HD), key_gain)
    k_flat = k_normed.reshape(TOKENS, HE)
    k_merged = (lax.optimization_barrier(jnp.sum(k_flat[merge_cells], axis=1)) * 0.25).astype(jnp.bfloat16)
    v_merged = (lax.optimization_barrier(jnp.sum(value_proj.astype(jnp.float32)[merge_cells], axis=1)) * 0.25).astype(jnp.bfloat16)
    results = lax.map(head_pass, (q_bf.transpose(1, 0, 2), by_head(k_merged, CELLS), by_head(v_merged, CELLS), by_head(grad_out, TOKENS)))
    attended = results[0].transpose(1, 0, 2).reshape(TOKENS, HE)
    grad_q_normed = results[1].transpose(1, 0, 2)
    grad_merged_k = results[2].transpose(1, 0, 2).reshape(CELLS, HE)
    grad_merged_v = results[3].transpose(1, 0, 2).reshape(CELLS, HE)
    grad_k_normed = (0.25 * grad_merged_k[unmerge]).reshape(TOKENS, H, HD)
    grad_value = (0.25 * grad_merged_v[unmerge]).astype(jnp.bfloat16)
    query_part = lax.optimization_barrier(jnp.sum(grad_q_normed * q_unit, axis=(0, 1)))
    key_part = lax.optimization_barrier(jnp.sum(grad_k_normed * k_unit, axis=(0, 1)))
    grad_query = norm_back(grad_q_normed, q_unit, q_scale, query_gain).reshape(TOKENS, HE).astype(jnp.bfloat16)
    grad_key = norm_back(grad_k_normed, k_unit, k_scale, key_gain).reshape(TOKENS, HE).astype(jnp.bfloat16)
    return (attended, grad_query, grad_key, grad_value, query_part, key_part)

def reference(query_proj, key_proj, value_proj, merge_cells, unmerge, grad_out, query_gain, key_gain):

    def image_pass(pieces):
        return one_image(pieces, query_gain, key_gain)
    results = lax.map(image_pass, (query_proj, key_proj, value_proj, merge_cells, unmerge, grad_out))
    return (results[0], results[1], results[2], results[3], lax.optimization_barrier(jnp.sum(results[4], axis=0)), lax.optimization_barrier(jnp.sum(results[5], axis=0)))
```

```python
import functools

import jax
import jax.numpy as jnp
from jax import lax
from jax.experimental import pallas as pl
from jax.experimental.pallas import tpu as pltpu
from jax.sharding import PartitionSpec as P

BF = jnp.bfloat16
F32 = jnp.float32
EPSILON = 1e-06
NZ, NX = 8, 4
HEADS = ((0, 1, 0, 0), (0, 1, 64, 64), (2, 3, 0, 0), (2, 3, 64, 64), (4, 4, 0, 64))


def dot(a, b):
    return jnp.dot(a, b, preferred_element_type=F32)


def dot_t(a, b):
    return lax.dot_general(a, b, (((1,), (1,)), ((), ())), preferred_element_type=F32)


def dot_l(a, b):
    return lax.dot_general(a, b, (((0,), (0,)), ((), ())), preferred_element_type=F32)


def split(value):
    high = value.astype(BF)
    return high, (value - high.astype(F32)).astype(BF)


def kernel(
    ny,
    q_in,
    k_in,
    v_in,
    merge_in,
    unmerge_in,
    g_in,
    q_gain,
    k_gain,
    att_out,
    gq_out,
    gk_out,
    gv_out,
    gain_out,
    q_unit,
    q_scale,
    k_unit,
    k_scale,
    kv_stage,
    qg_stage,
    kv,
    qg,
    qm,
    gm,
    q_t,
    g_t,
    es,
    acc,
    gq_acc,
    g_all,
    core_send,
    core_recv,
    up_send,
    up_recv,
    dn_send,
    dn_recv,
    out_stage,
    out_recv,
    cell_stage,
    cell_recv,
    gain_own,
    gain_core,
    gain_x,
    gain_y,
    gain_z,
    sem_xs,
    sem_xr,
    sem_us,
    sem_ur,
    sem_ds,
    sem_dr,
    sem_ps,
    sem_pr,
    sem_cs,
    sem_cr,
    sem_rus,
    sem_rur,
    sem_rds,
    sem_rdr,
    sem_gs,
    sem_gr,
):
    img = lax.axis_index("img")
    seq = lax.axis_index("seq")
    core = seq % 2
    x = (seq // 2) % NX
    z = seq // (2 * NX)
    other = 1 - core

    def at(zz, xx, cc):
        return (img, (zz * NX + xx) * 2 + cc)

    up = at((z + 1) % NZ, x, core)
    down = at((z + NZ - 1) % NZ, x, core)
    partner = at(z, x, other)
    x_peers = [at(z, (x + d) % NX, core) for d in range(1, NX)]
    z_peers = [at((z + d) % NZ, x, core) for d in range(1, NZ)]
    y_peers = [((img + d) % ny, seq) for d in range(1, ny)]
    barrier = pltpu.get_barrier_semaphore()
    greeted = [partner] + x_peers + z_peers + y_peers
    for device in greeted:
        pl.semaphore_signal(barrier, inc=1, device_id=device, device_id_type=pl.DeviceIdType.MESH)

    def remote(src, dst, send_sem, recv_sem, device):
        return pltpu.make_async_remote_copy(
            src_ref=src,
            dst_ref=dst,
            send_sem=send_sem,
            recv_sem=recv_sem,
            device_id=device,
            device_id_type=pl.DeviceIdType.MESH,
        )

    lane = lax.broadcasted_iota(jnp.int32, (1, 128), 1)
    low = lane < 64
    head_sum = (
        (lax.broadcasted_iota(jnp.int32, (128, 128), 0) < 64)
        == (lax.broadcasted_iota(jnp.int32, (128, 128), 1) < 64)
    ).astype(F32).astype(BF)

    def head_mean(value):
        high, rest = split(value)
        return (dot(high, head_sum) + dot(rest, head_sum)) * (1.0 / 64.0)

    gain_q = jnp.concatenate([q_gain[...], q_gain[...]], axis=1)
    gain_k = jnp.concatenate([k_gain[...], k_gain[...]], axis=1)
    token = seq * 128 + lane
    cells = merge_in[0]
    member = jnp.zeros((32, 128), F32)
    for j in range(4):
        member = member + (cells[:, j : j + 1] == token).astype(F32)
    member = member.astype(BF)

    def pick(first, second, which):
        if which == 0:
            return jnp.where(low, first, pltpu.roll(second, 64, 1)).astype(BF)
        return jnp.where(low, pltpu.roll(first, 64, 1), second).astype(BF)

    for pair in range(10):
        lanes = slice(pair * 128, pair * 128 + 128)
        raw = k_in[0, :, lanes].astype(F32)
        scale = lax.rsqrt(head_mean(raw * raw) + EPSILON)
        unit = raw * scale
        k_unit[:, lanes] = unit
        k_scale[:, lanes] = scale
        high, rest = split(unit * gain_k)
        merged_k = (dot(member, high) + dot(member, rest)) * 0.25
        merged_v = dot(member, v_in[0, :, lanes]) * 0.25
        if pair < 8:
            kv_stage[pair // 2, (pair % 2) * 2] = merged_k.astype(BF)
            kv_stage[pair // 2, (pair % 2) * 2 + 1] = merged_v.astype(BF)
        else:
            for which in range(2):
                kv_stage[(pair - 8) * 2 + which, 4] = pick(merged_k, merged_v, which)
    pl.semaphore_wait(barrier, len(greeted))

    def kv_x(d):
        return remote(
            kv_stage.at[(x + d) % NX],
            kv.at[:, z, core, pl.ds(pl.multiple_of(x * 32, 32), 32), :],
            sem_xs.at[0, d - 1],
            sem_xr.at[0, d - 1],
            x_peers[d - 1],
        )

    def qg_x(d):
        return remote(
            qg_stage.at[(x + d) % NX], qg.at[x], sem_xs.at[1, d - 1], sem_xr.at[1, d - 1], x_peers[d - 1]
        )

    for d in range(1, NX):
        kv_x(d).start()
    kv[:, z, core, pl.ds(pl.multiple_of(x * 32, 32), 32), :] = kv_stage[x]
    for pair in range(10):
        lanes = slice(pair * 128, pair * 128 + 128)
        raw = q_in[0, :, lanes].astype(F32)
        scale = lax.rsqrt(head_mean(raw * raw) + EPSILON)
        unit = raw * scale
        q_unit[:, lanes] = unit
        q_scale[:, lanes] = scale
        normed = (unit * gain_q).astype(BF).astype(F32) * 0.125
        if pair < 8:
            qg_stage[pair // 2, (pair % 2) * 2] = normed.astype(BF)
            qg_stage[pair // 2, (pair % 2) * 2 + 1] = g_in[0, :, lanes]
        else:
            upstream = g_in[0, :, lanes].astype(F32)
            for which in range(2):
                qg_stage[(pair - 8) * 2 + which, 4] = pick(normed, upstream, which)
    for d in range(1, NX):
        qg_x(d).start()
    qg[x] = qg_stage[x]

    def z_slot(offset):
        return (z + offset + NZ) % NZ

    def ag_up(s):
        ref = kv.at[:, z_slot(1 - s), core]
        return remote(ref, ref, sem_us.at[s - 1], sem_ur.at[s - 1], up)

    def ag_down(s):
        ref = kv.at[:, z_slot(s - 1), core]
        return remote(ref, ref, sem_ds.at[s - 1], sem_dr.at[s - 1], down)

    def ag_partner(i, offset):
        ref = kv.at[:, z_slot(offset), core]
        return remote(ref, ref, sem_ps.at[i], sem_pr.at[i], partner)

    for d in range(1, NX):
        kv_x(d).wait_recv()
    ag_up(1).start()
    ag_down(1).start()
    ag_partner(0, 0).start()

    def head_blocks(h):
        single = (h == 4).astype(jnp.int32)
        base = (h // 2) * 2
        q_block = base
        g_block = base + 1 - single
        q_lane = (h % 2) * 64
        g_lane = q_lane + 64 * single
        return q_block, g_block, pl.multiple_of(q_lane, 64), pl.multiple_of(g_lane, 64)

    def cell_rows(block, first, second):
        return jnp.concatenate(
            [kv[block, first].reshape(256, 128), kv[block, second].reshape(256, 128)], axis=0
        )

    def value_rows(block, g_lane, first, second):
        rows = cell_rows(block, first, second)
        mine = (lane < 64) == (g_lane < 64)
        return jnp.where(mine, rows, jnp.ones_like(rows))

    def forward(first, second):
        def body(h, carry):
            q_block, g_block, q_lane, g_lane = head_blocks(h)
            scores = dot_t(qm[h], cell_rows(q_block, first, second))
            weights = jnp.exp(scores).astype(BF)
            es[h, first] = weights[:, :256]
            es[h, second] = weights[:, 256:]
            acc[h] += dot(weights, value_rows(g_block, g_lane, first, second))
            return carry

        lax.fori_loop(0, 5, body, 0)

    def forward_pair(s):
        forward(z_slot(-s), z_slot(s - 1))

    def wait_partner(indices):
        for i in indices:
            ag_partner(i, 0).wait_recv()

    acc[...] = jnp.zeros_like(acc)
    gq_acc[...] = jnp.zeros_like(gq_acc)
    for s in range(1, 5):
        ag_up(s).wait_recv()
        if s < 4:
            ag_up(s + 1).start()
        ag_partner(2 * s - 1, -s).start()
        if s < 4:
            ag_down(s).wait_recv()
            if s < 3:
                ag_down(s + 1).start()
            ag_partner(2 * s, s).start()
        if s == 1:
            for d in range(1, NX):
                qg_x(d).wait_recv()
            for h, (q_block, g_block, q_lane, g_lane) in enumerate(HEADS):
                rows = qg[:, q_block].reshape(512, 128)
                qm[h] = jnp.where(low == (q_lane < 64), rows, jnp.zeros_like(rows))
        if s == 2:
            wait_partner((0, 1))
            forward_pair(1)
        if s == 3:
            wait_partner((2, 3))
            forward_pair(2)
            wait_partner((4, 5))
            forward_pair(3)
        if s == 4:
            wait_partner((6, 7))
            forward_pair(4)

    attended = []
    for h, (q_block, g_block, q_lane, g_lane) in enumerate(HEADS):
        mine = low == (g_lane < 64)
        total = acc[h]
        inverse = pltpu.roll(1.0 / total, 64, 1)
        weighted = jnp.where(mine, total * inverse, 0.0).astype(BF)
        scaled = jnp.where(mine, qg[:, g_block].reshape(512, 128).astype(F32) * inverse, 0.0).astype(BF)
        inner = jnp.sum(scaled.astype(F32) * weighted.astype(F32), axis=1, keepdims=True)
        high, rest = split(inner)
        spare = 64 - g_lane
        gm[h] = jnp.where(
            mine,
            scaled,
            jnp.where(lane == spare, -high, jnp.where(lane == spare + 1, -rest, jnp.zeros_like(scaled))),
        )
        q_t[h] = jnp.transpose(qm[h].astype(F32))[q_lane : q_lane + 64].astype(BF)
        g_t[h] = jnp.transpose(scaled.astype(F32))[g_lane : g_lane + 64].astype(BF)
        if h == 0 or h == 2:
            held = weighted
        elif h == 4:
            out_stage[:, 4] = weighted.reshape(4, 128, 128)
        else:
            out_stage[:, h // 2] = jnp.where(low, held, weighted).reshape(4, 128, 128)

    def out_x(part, d):
        blocks = pl.ds(0, 2) if part == 0 else pl.ds(2, 3)
        return remote(
            out_stage.at[(x + d) % NX, blocks],
            out_recv.at[x, blocks],
            sem_xs.at[2 + part, d - 1],
            sem_xr.at[2 + part, d - 1],
            x_peers[d - 1],
        )

    for d in range(1, NX):
        out_x(0, d).start()

    def backward(step, first, second, start, stop):
        def body(h, carry):
            q_block, g_block, q_lane, g_lane = head_blocks(h)
            keys = cell_rows(q_block, first, second)
            weights = jnp.concatenate([es[h, first], es[h, second]], axis=1)
            change = dot_t(gm[h], value_rows(g_block, g_lane, first, second))
            grads = (change * weights.astype(F32)).astype(BF)
            gq_acc[h] += dot(grads, keys)
            key_part = dot(q_t[h], grads)
            value_part = dot(g_t[h], weights)
            for i in range(2):
                for c in range(2):
                    cols = slice(i * 256 + c * 128, i * 256 + c * 128 + 128)
                    g_all[step, i, c, q_block, pl.ds(q_lane, 64), :] = key_part[:, cols]
                    g_all[step, i, c, g_block, pl.ds(g_lane, 64), :] = value_part[:, cols]
            return carry

        lax.fori_loop(start, stop, body, 0)

    def core_copy(step):
        return remote(core_send.at[step], core_recv.at[step], sem_cs.at[step], sem_cr.at[step], partner)

    def rs_up(step):
        return remote(up_send.at[step], up_recv.at[step], sem_rus.at[step], sem_rur.at[step], up)

    def rs_down(step):
        return remote(dn_send.at[step], dn_recv.at[step], sem_rds.at[step], sem_rdr.at[step], down)

    def reduce_step(step):
        core_copy(step).wait_recv()
        upward = g_all[step, 0, core] + core_recv[step, 0].astype(F32)
        if step > 0:
            rs_up(step - 1).wait_recv()
            upward = upward + up_recv[step - 1].astype(F32)
        up_send[step] = upward.astype(BF)
        rs_up(step).start()
        if step < 3:
            downward = g_all[step, 1, core] + core_recv[step, 1].astype(F32)
            if step > 0:
                rs_down(step - 1).wait_recv()
                downward = downward + dn_recv[step - 1].astype(F32)
            dn_send[step] = downward.astype(BF)
            rs_down(step).start()

    for step in range(4):
        first, second = z_slot(4 - step), z_slot(step - 3)
        if step == 0:
            backward(step, first, second, 0, 5)
        else:
            backward(step, first, second, 0, 3)
            reduce_step(step - 1)
            backward(step, first, second, 3, 5)
        core_send[step] = g_all[step, :, other].astype(BF)
        core_copy(step).start()

    for h in (0, 2):
        out_stage[:, 2 + h // 2] = (
            jnp.where(low, gq_acc[h], gq_acc[h + 1]).astype(BF).reshape(4, 128, 128)
        )
    out_stage[:, 4] = jnp.where(
        low, gq_acc[4], out_stage[:, 4].reshape(512, 128).astype(F32)
    ).astype(BF).reshape(4, 128, 128)
    for d in range(1, NX):
        out_x(1, d).start()
    out_recv[x] = out_stage[x]
    reduce_step(3)

    for part in range(2):
        for d in range(1, NX):
            out_x(part, d).wait_recv()

    def join(first, second, which):
        if which == 0:
            return jnp.where(low, first, pltpu.roll(second, 64, 1))
        return jnp.where(low, pltpu.roll(first, 64, 1), second)

    q_terms = jnp.zeros((8, 128), F32)
    for pair in range(10):
        lanes = slice(pair * 128, pair * 128 + 128)
        if pair < 8:
            att_out[0, :, lanes] = out_recv[pair // 2, pair % 2]
            grad = out_recv[pair // 2, 2 + pair % 2].astype(F32)
        else:
            one = out_recv[(pair - 8) * 2, 4].astype(F32)
            two = out_recv[(pair - 8) * 2 + 1, 4].astype(F32)
            att_out[0, :, lanes] = join(one, two, 1).astype(BF)
            grad = join(one, two, 0)
        grad = grad * 0.125
        unit = q_unit[:, lanes]
        product = grad * unit
        q_terms = q_terms + jnp.sum(product.reshape(16, 8, 128), axis=0)
        inner = head_mean(product * gain_q)
        gq_out[0, :, lanes] = (q_scale[:, lanes] * (grad * gain_q - unit * inner)).astype(BF)

    rs_up(3).wait_recv()
    rs_down(2).wait_recv()
    for b in range(5):
        final = (
            g_all[3, 1, core, b]
            + core_recv[3, 1, b].astype(F32)
            + up_recv[3, b].astype(F32)
            + dn_recv[2, b].astype(F32)
        )
        cell_stage[b] = jnp.transpose(final).astype(BF)

    def cell_x(d):
        rows = pl.ds(pl.multiple_of(((x + d) % NX) * 32, 32), 32)
        return remote(
            cell_stage.at[:, rows, :], cell_recv.at[x], sem_xs.at[4, d - 1], sem_xr.at[4, d - 1], x_peers[d - 1]
        )

    for d in range(1, NX):
        cell_x(d).start()
    cell_recv[x] = cell_stage[:, pl.ds(pl.multiple_of(x * 32, 32), 32), :]
    cell = seq * 32 + lax.broadcasted_iota(jnp.int32, (32, 1), 0)
    table = (unmerge_in[...] == cell).astype(F32).astype(BF)
    for d in range(1, NX):
        cell_x(d).wait_recv()

    k_terms = jnp.zeros((8, 128), F32)
    for pair in range(10):
        lanes = slice(pair * 128, pair * 128 + 128)
        if pair < 8:
            cell_k = cell_recv[pair // 2, (pair % 2) * 2]
            cell_v = cell_recv[pair // 2, (pair % 2) * 2 + 1]
        else:
            one = cell_recv[(pair - 8) * 2, 4].astype(F32)
            two = cell_recv[(pair - 8) * 2 + 1, 4].astype(F32)
            cell_k = join(one, two, 0).astype(BF)
            cell_v = join(one, two, 1).astype(BF)
        gv_out[0, :, lanes] = (dot_l(table, cell_v) * 0.25).astype(BF)
        grad = dot_l(table, cell_k) * 0.25
        unit = k_unit[:, lanes]
        product = grad * unit
        k_terms = k_terms + jnp.sum(product.reshape(16, 8, 128), axis=0)
        inner = head_mean(product * gain_k)
        gk_out[0, :, lanes] = (k_scale[:, lanes] * (grad * gain_k - unit * inner)).astype(BF)

    q_row = jnp.sum(q_terms, axis=0, keepdims=True)
    k_row = jnp.sum(k_terms, axis=0, keepdims=True)
    q_row = q_row + pltpu.roll(q_row, 64, 1)
    k_row = k_row + pltpu.roll(k_row, 64, 1)
    value = jnp.broadcast_to(jnp.where(low, q_row, k_row), (8, 128))

    def total_over(value, slot, stage, base, buffer, mine, peers, count):
        gain_own[stage] = value
        copies = []
        for i, device in enumerate(peers):
            copies.append(
                remote(
                    gain_own.at[stage], buffer.at[mine], sem_gs.at[base + i], sem_gr.at[base + i], device
                )
            )
        for copy in copies:
            copy.start()
        buffer[mine] = value
        for copy in copies:
            copy.wait_recv()
        result = buffer[0]
        for i in range(1, count):
            result = result + buffer[i]
        return result

    value = total_over(value, core, 0, 0, gain_core, core, [partner], 2)
    value = total_over(value, x, 1, 1, gain_x, x, x_peers, NX)
    if ny > 1:
        value = total_over(value, img, 2, 4, gain_y, img, y_peers, ny)
    value = total_over(value, z, 3, 7, gain_z, z, z_peers, NZ)
    gain_out[...] = value

    for d in range(1, NX):
        kv_x(d).wait_send()
        qg_x(d).wait_send()
        out_x(0, d).wait_send()
        out_x(1, d).wait_send()
        cell_x(d).wait_send()
    for s in range(1, 5):
        ag_up(s).wait_send()
        if s < 4:
            ag_down(s).wait_send()
    for i in range(8):
        ag_partner(i, 0).wait_send()
    for step in range(4):
        core_copy(step).wait_send()
        rs_up(step).wait_send()
        if step < 3:
            rs_down(step).wait_send()
    tile = gain_own.at[0]
    for i in range(1 + (NX - 1) + (ny - 1) + (NZ - 1)):
        slot = i if ny > 1 or i < 4 else i + 3
        remote(tile, tile, sem_gs.at[slot], sem_gr.at[slot], partner).wait_send()


def local(ny, query_proj, key_proj, value_proj, merge_cells, unmerge, grad_out, query_gain, key_gain):
    vmem = pltpu.VMEM
    dma = pltpu.SemaphoreType.DMA
    block = (5, 128, 128)
    outs = pl.pallas_call(
        functools.partial(kernel, ny),
        out_shape=[jax.ShapeDtypeStruct((1, 128, 1280), BF)] * 4
        + [jax.ShapeDtypeStruct((8, 128), F32)],
        in_specs=[pl.BlockSpec(memory_space=pltpu.VMEM)] * 8,
        out_specs=[pl.BlockSpec(memory_space=pltpu.VMEM)] * 5,
        scratch_shapes=[
            vmem((128, 1280), F32),
            vmem((128, 1280), F32),
            vmem((128, 1280), F32),
            vmem((128, 1280), F32),
            vmem((4, 5, 32, 128), BF),
            vmem((4,) + block, BF),
            vmem((5, 8, 2, 128, 128), BF),
            vmem((4,) + block, BF),
            vmem((5, 512, 128), BF),
            vmem((5, 512, 128), BF),
            vmem((5, 64, 512), BF),
            vmem((5, 64, 512), BF),
            vmem((5, 8, 512, 256), BF),
            vmem((5, 512, 128), F32),
            vmem((5, 512, 128), F32),
            vmem((4, 2, 2) + block, F32),
            vmem((4, 2) + block, BF),
            vmem((4, 2) + block, BF),
            vmem((4,) + block, BF),
            vmem((4,) + block, BF),
            vmem((3,) + block, BF),
            vmem((3,) + block, BF),
            vmem((4,) + block, BF),
            vmem((4,) + block, BF),
            vmem(block, BF),
            vmem((4, 5, 32, 128), BF),
            vmem((4, 8, 128), F32),
            vmem((2, 8, 128), F32),
            vmem((NX, 8, 128), F32),
            vmem((max(ny, 2), 8, 128), F32),
            vmem((NZ, 8, 128), F32),
            dma((5, 3)),
            dma((5, 3)),
            dma((4,)),
            dma((4,)),
            dma((3,)),
            dma((3,)),
            dma((8,)),
            dma((8,)),
            dma((4,)),
            dma((4,)),
            dma((4,)),
            dma((4,)),
            dma((3,)),
            dma((3,)),
            dma((14,)),
            dma((14,)),
        ],
        compiler_params=pltpu.CompilerParams(
            collective_id=0, has_side_effects=True, vmem_limit_bytes=60 * 1024 * 1024
        ),
        name="attention_block",
    )(
        query_proj,
        key_proj,
        value_proj,
        merge_cells,
        unmerge,
        grad_out,
        query_gain.reshape(1, 64),
        key_gain.reshape(1, 64),
    )
    return (outs[0], outs[1], outs[2], outs[3], outs[4][0, :64], outs[4][0, 64:])


def solution(mesh):
    placed = (
        P("img", "seq", None),
        P("img", "seq", None),
        P("img", "seq", None),
        P("img", "seq", None),
        P("img", "seq"),
        P("img", "seq", None),
        P(),
        P(),
    )
    return jax.shard_map(
        functools.partial(local, mesh.shape["img"]),
        mesh=mesh,
        in_specs=placed,
        out_specs=(
            P("img", "seq", None),
            P("img", "seq", None),
            P("img", "seq", None),
            P("img", "seq", None),
            P(),
            P(),
        ),
        check_vma=False,
    )
```

```python
import functools

import jax
import jax.numpy as jnp
from jax import lax
from jax.experimental import pallas as pl
from jax.experimental.pallas import tpu as pltpu
from jax.sharding import PartitionSpec as P

BF = jnp.bfloat16
F32 = jnp.float32
EPSILON = 1e-06
NZ, NX = 8, 4
HEADS = ((0, 1, 0, 0), (0, 1, 64, 64), (2, 3, 0, 0), (2, 3, 64, 64), (4, 4, 0, 64))
Q_AT = {0: 0, 2: 1, 4: 2, 1: 3, 3: 4}
PARTS = ((0, 2), (2, 3))


def dot(a, b):
    return jnp.dot(a, b, preferred_element_type=F32)


def dot_t(a, b):
    return lax.dot_general(a, b, (((1,), (1,)), ((), ())), preferred_element_type=F32)


def dot_l(a, b):
    return lax.dot_general(a, b, (((0,), (0,)), ((), ())), preferred_element_type=F32)


def split(value):
    high = value.astype(BF)
    return high, (value - high.astype(F32)).astype(BF)


def kernel(
    ny,
    q_in,
    k_in,
    v_in,
    unmerge_in,
    g_in,
    q_gain,
    k_gain,
    att_out,
    gq_out,
    gk_out,
    gv_out,
    gain_out,
    q_unit,
    q_scale,
    k_unit,
    k_scale,
    kv_stage,
    qg_stage,
    kv,
    qg,
    qm,
    gm,
    q_t,
    g_t,
    es,
    acc,
    gq_acc,
    g_all,
    core_send,
    core_recv,
    up_send,
    up_recv,
    dn_send,
    dn_recv,
    out_stage,
    out_recv,
    cell_stage,
    cell_recv,
    gain_own,
    gain_core,
    gain_x,
    gain_y,
    gain_z,
    sem_xs,
    sem_xr,
    sem_us,
    sem_ur,
    sem_ds,
    sem_dr,
    sem_ps,
    sem_pr,
    sem_cs,
    sem_cr,
    sem_rus,
    sem_rur,
    sem_rds,
    sem_rdr,
    sem_gs,
    sem_gr,
):
    img = lax.axis_index("img")
    seq = lax.axis_index("seq")
    core = seq % 2
    x = (seq // 2) % NX
    z = seq // (2 * NX)
    other = 1 - core

    def at(zz, xx, cc):
        return (img, (zz * NX + xx) * 2 + cc)

    up = at((z + 1) % NZ, x, core)
    down = at((z + NZ - 1) % NZ, x, core)
    partner = at(z, x, other)
    x_peers = [at(z, (x + d) % NX, core) for d in range(1, NX)]
    z_peers = [at((z + d) % NZ, x, core) for d in range(1, NZ)]
    y_peers = [((img + d) % ny, seq) for d in range(1, ny)]
    barrier = pltpu.get_barrier_semaphore()
    greeted = [partner] + x_peers + z_peers + y_peers
    for device in greeted:
        pl.semaphore_signal(barrier, inc=1, device_id=device, device_id_type=pl.DeviceIdType.MESH)

    def remote(src, dst, send_sem, recv_sem, device):
        return pltpu.make_async_remote_copy(
            src_ref=src,
            dst_ref=dst,
            send_sem=send_sem,
            recv_sem=recv_sem,
            device_id=device,
            device_id_type=pl.DeviceIdType.MESH,
        )

    lane = lax.broadcasted_iota(jnp.int32, (1, 128), 1)
    low = lane < 64
    head_sum = (
        (lax.broadcasted_iota(jnp.int32, (128, 128), 0) < 64)
        == (lax.broadcasted_iota(jnp.int32, (128, 128), 1) < 64)
    ).astype(F32).astype(BF)

    def head_mean(value):
        high, rest = split(value)
        return (dot(high, head_sum) + dot(rest, head_sum)) * (1.0 / 64.0)

    gain_q = jnp.concatenate([q_gain[...], q_gain[...]], axis=1)
    gain_k = jnp.concatenate([k_gain[...], k_gain[...]], axis=1)
    cell = seq * 32 + lax.broadcasted_iota(jnp.int32, (32, 1), 0)
    member = (unmerge_in[...] == cell).astype(F32).astype(BF)

    def pick(first, second, which):
        if which == 0:
            return jnp.where(low, first, pltpu.roll(second, 64, 1)).astype(BF)
        return jnp.where(low, pltpu.roll(first, 64, 1), second).astype(BF)

    for pair in range(10):
        lanes = slice(pair * 128, pair * 128 + 128)
        raw = k_in[0, :, lanes].astype(F32)
        scale = lax.rsqrt(head_mean(raw * raw) + EPSILON)
        unit = raw * scale
        k_unit[:, lanes] = unit
        k_scale[:, lanes] = scale
        high, rest = split(unit * gain_k)
        merged_k = (dot(member, high) + dot(member, rest)) * 0.25
        merged_v = dot(member, v_in[0, :, lanes]) * 0.25
        if pair < 8:
            kv_stage[pair // 2, (pair % 2) * 2] = merged_k.astype(BF)
            kv_stage[pair // 2, (pair % 2) * 2 + 1] = merged_v.astype(BF)
        else:
            for which in range(2):
                kv_stage[(pair - 8) * 2 + which, 4] = pick(merged_k, merged_v, which)
    pl.semaphore_wait(barrier, len(greeted))

    def kv_x(d):
        return remote(
            kv_stage.at[(x + d) % NX],
            kv.at[:, z, core, pl.ds(pl.multiple_of(x * 32, 32), 32), :],
            sem_xs.at[0, d - 1],
            sem_xr.at[0, d - 1],
            x_peers[d - 1],
        )

    def qg_x(part, d):
        blocks = pl.ds(0, 3) if part == 0 else pl.ds(3, 2)
        return remote(
            qg_stage.at[(x + d) % NX, blocks],
            qg.at[x, blocks],
            sem_xs.at[1 + part, d - 1],
            sem_xr.at[1 + part, d - 1],
            x_peers[d - 1],
        )

    for d in range(1, NX):
        kv_x(d).start()
    kv[:, z, core, pl.ds(pl.multiple_of(x * 32, 32), 32), :] = kv_stage[x]
    for pair in range(10):
        lanes = slice(pair * 128, pair * 128 + 128)
        raw = q_in[0, :, lanes].astype(F32)
        scale = lax.rsqrt(head_mean(raw * raw) + EPSILON)
        unit = raw * scale
        q_unit[:, lanes] = unit
        q_scale[:, lanes] = scale
        normed = (unit * gain_q).astype(BF).astype(F32) * 0.125
        if pair < 8:
            qg_stage[pair // 2, pair % 2] = normed.astype(BF)
        else:
            upstream = g_in[0, :, lanes].astype(F32)
            for which in range(2):
                qg_stage[(pair - 8) * 2 + which, 2] = pick(normed, upstream, which)
    for d in range(1, NX):
        qg_x(0, d).start()
    for pair in range(8):
        qg_stage[pair // 2, 3 + pair % 2] = g_in[0, :, pair * 128 : pair * 128 + 128]
    for d in range(1, NX):
        qg_x(1, d).start()
    qg[x] = qg_stage[x]

    def z_slot(offset):
        return (z + offset + NZ) % NZ

    def blocks_of(part):
        return pl.ds(*PARTS[part])

    def ag_up(s, part):
        ref = kv.at[blocks_of(part), z_slot(1 - s), core]
        return remote(ref, ref, sem_us.at[s - 1, part], sem_ur.at[s - 1, part], up)

    def ag_down(s, part):
        ref = kv.at[blocks_of(part), z_slot(s - 1), core]
        return remote(ref, ref, sem_ds.at[s - 1, part], sem_dr.at[s - 1, part], down)

    def ag_partner(i, offset, part):
        ref = kv.at[blocks_of(part), z_slot(offset), core]
        return remote(ref, ref, sem_ps.at[i, part], sem_pr.at[i, part], partner)

    def on_up(s, part):
        return s < 4 or part == 0

    def on_down(s, part):
        return s < 4 or part == 1

    def gather_hop(s, part):
        if on_up(s, part):
            ag_up(s, part).wait_recv()
            if s < 4 and on_up(s + 1, part):
                ag_up(s + 1, part).start()
            ag_partner(2 * s - 1, -s, part).start()
        if on_down(s, part):
            ag_down(s, part).wait_recv()
            if s < 4 and on_down(s + 1, part):
                ag_down(s + 1, part).start()
            ag_partner(2 * s if s < 4 else 7, s, part).start()

    for d in range(1, NX):
        kv_x(d).wait_recv()
    for part in range(2):
        ag_up(1, part).start()
        ag_down(1, part).start()
    for part in range(2):
        ag_partner(0, 0, part).start()

    def head_blocks(h):
        single = (h == 4).astype(jnp.int32)
        base = (h // 2) * 2
        q_block = base
        g_block = base + 1 - single
        q_lane = (h % 2) * 64
        g_lane = q_lane + 64 * single
        return q_block, g_block, pl.multiple_of(q_lane, 64), pl.multiple_of(g_lane, 64)

    def cell_rows(block, first, second):
        return jnp.concatenate(
            [kv[block, first].reshape(256, 128), kv[block, second].reshape(256, 128)], axis=0
        )

    def value_rows(block, g_lane, first, second):
        rows = cell_rows(block, first, second)
        mine = (lane < 64) == (g_lane < 64)
        return jnp.where(mine, rows, jnp.ones_like(rows))

    def forward(first, second, start, stop):
        def body(h, carry):
            q_block, g_block, q_lane, g_lane = head_blocks(h)
            scores = dot_t(qm[h], cell_rows(q_block, first, second))
            weights = jnp.exp(scores).astype(BF)
            es[h, first] = weights[:, :256]
            es[h, second] = weights[:, 256:]
            acc[h] += dot(weights, value_rows(g_block, g_lane, first, second))
            return carry

        lax.fori_loop(start, stop, body, 0)

    def forward_pair(s, start, stop):
        forward(z_slot(-s), z_slot(s - 1), start, stop)

    def wait_partner(indices):
        for i in indices:
            for part in range(2):
                ag_partner(i, 0, part).wait_recv()

    acc[...] = jnp.zeros_like(acc)
    gq_acc[...] = jnp.zeros_like(gq_acc)
    gather_hop(1, 0)
    gather_hop(1, 1)
    for d in range(1, NX):
        qg_x(0, d).wait_recv()
    for h, (q_block, g_block, q_lane, g_lane) in enumerate(HEADS):
        rows = qg[:, Q_AT[q_block]].reshape(512, 128)
        qm[h] = jnp.where(low == (q_lane < 64), rows, jnp.zeros_like(rows))
        if h == 1:
            gather_hop(2, 0)
    wait_partner((0, 1))
    forward_pair(1, 0, 2)
    gather_hop(2, 1)
    forward_pair(1, 2, 5)
    gather_hop(3, 0)
    wait_partner((2, 3))
    forward_pair(2, 0, 2)
    gather_hop(3, 1)
    forward_pair(2, 2, 5)
    gather_hop(4, 0)
    gather_hop(4, 1)
    for h, (q_block, g_block, q_lane, g_lane) in enumerate(HEADS):
        q_t[h] = jnp.transpose(qm[h].astype(F32))[q_lane : q_lane + 64].astype(BF)
    wait_partner((4, 5))
    forward_pair(3, 0, 5)
    wait_partner((6, 7))
    forward_pair(4, 0, 5)
    for d in range(1, NX):
        qg_x(1, d).wait_recv()

    attended = []
    for h, (q_block, g_block, q_lane, g_lane) in enumerate(HEADS):
        mine = low == (g_lane < 64)
        total = acc[h]
        inverse = pltpu.roll(1.0 / total, 64, 1)
        weighted = jnp.where(mine, total * inverse, 0.0).astype(BF)
        scaled = jnp.where(mine, qg[:, Q_AT[g_block]].reshape(512, 128).astype(F32) * inverse, 0.0).astype(BF)
        inner = jnp.sum(scaled.astype(F32) * weighted.astype(F32), axis=1, keepdims=True)
        high, rest = split(inner)
        spare = 64 - g_lane
        gm[h] = jnp.where(
            mine,
            scaled,
            jnp.where(lane == spare, -high, jnp.where(lane == spare + 1, -rest, jnp.zeros_like(scaled))),
        )
        g_t[h] = jnp.transpose(scaled.astype(F32))[g_lane : g_lane + 64].astype(BF)
        if h == 0 or h == 2:
            held = weighted
        elif h == 4:
            out_stage[:, 4] = weighted.reshape(4, 128, 128)
        else:
            out_stage[:, h // 2] = jnp.where(low, held, weighted).reshape(4, 128, 128)

    def out_x(part, d):
        blocks = pl.ds(*((0, 2), (2, 1), (3, 2))[part])
        return remote(
            out_stage.at[(x + d) % NX, blocks],
            out_recv.at[x, blocks],
            sem_xs.at[3 + part, d - 1],
            sem_xr.at[3 + part, d - 1],
            x_peers[d - 1],
        )

    for d in range(1, NX):
        out_x(0, d).start()

    def backward(step, first, second, start, stop):
        def body(h, carry):
            q_block, g_block, q_lane, g_lane = head_blocks(h)
            keys = cell_rows(q_block, first, second)
            weights = jnp.concatenate([es[h, first], es[h, second]], axis=1)
            change = dot_t(gm[h], value_rows(g_block, g_lane, first, second))
            grads = (change * weights.astype(F32)).astype(BF)
            gq_acc[h] += dot(grads, keys)
            key_part = dot(q_t[h], grads)
            value_part = dot(g_t[h], weights)
            for i in range(2):
                for c in range(2):
                    cols = slice(i * 256 + c * 128, i * 256 + c * 128 + 128)
                    g_all[step, i, c, q_block, pl.ds(q_lane, 64), :] = key_part[:, cols]
                    g_all[step, i, c, g_block, pl.ds(g_lane, 64), :] = value_part[:, cols]
            return carry

        lax.fori_loop(start, stop, body, 0)

    def core_copy(step, part):
        blocks = blocks_of(part)
        return remote(
            core_send.at[step, :, blocks],
            core_recv.at[step, :, blocks],
            sem_cs.at[step, part],
            sem_cr.at[step, part],
            partner,
        )

    def rs_up(hop, part):
        blocks = blocks_of(part)
        return remote(
            up_send.at[hop, blocks], up_recv.at[hop, blocks], sem_rus.at[hop, part], sem_rur.at[hop, part], up
        )

    def rs_down(hop, part):
        blocks = blocks_of(part)
        return remote(
            dn_send.at[hop, blocks], dn_recv.at[hop, blocks], sem_rds.at[hop, part], sem_rdr.at[hop, part], down
        )

    def chip_sum(step, i, part):
        blocks = blocks_of(part)
        return g_all[step, i, core, blocks] + core_recv[step, i, blocks].astype(F32)

    def send_up(hop, step, i, part):
        value = chip_sum(step, i, part)
        blocks = blocks_of(part)
        if hop > 0 and not (hop == 1 and part == 1):
            rs_up(hop - 1, part).wait_recv()
            value = value + up_recv[hop - 1, blocks].astype(F32)
        up_send[hop, blocks] = value.astype(BF)
        rs_up(hop, part).start()

    def send_down(hop, step, i, part):
        value = chip_sum(step, i, part)
        blocks = blocks_of(part)
        if hop > 0 and not (hop == 1 and part == 0):
            rs_down(hop - 1, part).wait_recv()
            value = value + dn_recv[hop - 1, blocks].astype(F32)
        dn_send[hop, blocks] = value.astype(BF)
        rs_down(hop, part).start()

    def reduce_half(step, part):
        core_copy(step, part).wait_recv()
        if step == 0 and part == 0:
            send_up(0, 0, 0, 0)
        elif step == 0:
            send_down(0, 0, 0, 1)
            send_up(1, 0, 1, 1)
        elif step == 1 and part == 0:
            send_down(1, 1, 0, 0)
            send_up(1, 0, 1, 0)
        elif step < 3:
            if step == 2 and part == 0:
                send_up(2, 1, 1, 0)
            send_down(step, step, 0, part)
            if part == 1:
                send_up(step + 1, step, 1, 1)
        else:
            if part == 0:
                send_up(3, 2, 1, 0)
            send_down(3, 3, 0, part)

    def backward_half(step, part):
        first = z_slot((4, -3, -2, -1)[step])
        second = z_slot((3, 2, 1, 0)[step])
        backward(step, first, second, *((0, 2), (2, 5))[part])
        blocks = blocks_of(part)
        core_send[step, :, blocks] = g_all[step, :, other, blocks].astype(BF)
        core_copy(step, part).start()

    for step in range(4):
        backward_half(step, 0)
        if step > 0:
            reduce_half(step - 1, 1)
        if step == 3:
            out_stage[:, 2] = jnp.where(low, gq_acc[0], gq_acc[1]).astype(BF).reshape(4, 128, 128)
            for d in range(1, NX):
                out_x(1, d).start()
        backward_half(step, 1)
        reduce_half(step, 0)

    out_stage[:, 3] = jnp.where(low, gq_acc[2], gq_acc[3]).astype(BF).reshape(4, 128, 128)
    out_stage[:, 4] = (
        jnp.where(low, gq_acc[4], out_stage[:, 4].reshape(512, 128).astype(F32))
        .astype(BF)
        .reshape(4, 128, 128)
    )
    for d in range(1, NX):
        out_x(2, d).start()
    out_recv[x] = out_stage[x]
    reduce_half(3, 1)

    def gain_copies(stage):
        base, buffer, mine, peers = gain_stages[stage]
        return [
            remote(gain_own.at[stage], buffer.at[mine], sem_gs.at[base + i], sem_gr.at[base + i], device)
            for i, device in enumerate(peers)
        ]

    def gain_send(stage, value):
        base, buffer, mine, peers = gain_stages[stage]
        gain_own[stage] = value
        for copy in gain_copies(stage):
            copy.start()
        buffer[mine] = value

    def gain_sum(stage):
        base, buffer, mine, peers = gain_stages[stage]
        for copy in gain_copies(stage):
            copy.wait_recv()
        result = buffer[0]
        for i in range(1, len(peers) + 1):
            result = result + buffer[i]
        return result

    gain_stages = (
        (0, gain_core, core, [partner]),
        (1, gain_x, x, x_peers),
        (4, gain_y, img, y_peers),
        (7, gain_z, z, z_peers),
    )
    tile = jnp.zeros((8, 128), F32)
    for h in range(5):
        tile = tile + jnp.sum((qm[h].astype(F32) * gq_acc[h]).reshape(64, 8, 128), axis=0)
    gain_send(0, tile)

    def join(first, second, which):
        if which == 0:
            return jnp.where(low, first, pltpu.roll(second, 64, 1))
        return jnp.where(low, pltpu.roll(first, 64, 1), second)

    def final_sum():
        for part in range(2):
            rs_up(3, part).wait_recv()
            rs_down(3, part).wait_recv()
        for b in range(5):
            total = (
                g_all[3, 1, core, b]
                + core_recv[3, 1, b].astype(F32)
                + up_recv[3, b].astype(F32)
                + dn_recv[3, b].astype(F32)
            )
            cell_stage[b] = jnp.transpose(total).astype(BF)

    def cell_x(d):
        rows = pl.ds(pl.multiple_of(((x + d) % NX) * 32, 32), 32)
        return remote(
            cell_stage.at[:, rows, :], cell_recv.at[x], sem_xs.at[6, d - 1], sem_xr.at[6, d - 1], x_peers[d - 1]
        )

    for d in range(1, NX):
        out_x(0, d).wait_recv()
    for pair in range(8):
        att_out[0, :, pair * 128 : pair * 128 + 128] = out_recv[pair // 2, pair % 2]
    gain_send(1, gain_sum(0))
    final_sum()
    for d in range(1, NX):
        cell_x(d).start()
    cell_recv[x] = cell_stage[:, pl.ds(pl.multiple_of(x * 32, 32), 32), :]
    gain_send(2, gain_sum(1))

    for part in (1, 2):
        for d in range(1, NX):
            out_x(part, d).wait_recv()
    for pair in range(10):
        lanes = slice(pair * 128, pair * 128 + 128)
        if pair < 8:
            grad = out_recv[pair // 2, 2 + pair % 2].astype(F32)
        else:
            one = out_recv[(pair - 8) * 2, 4].astype(F32)
            two = out_recv[(pair - 8) * 2 + 1, 4].astype(F32)
            att_out[0, :, lanes] = join(one, two, 1).astype(BF)
            grad = join(one, two, 0)
        grad = grad * 0.125 * gain_q
        unit = q_unit[:, lanes]
        inner = head_mean(grad * unit)
        gq_out[0, :, lanes] = (q_scale[:, lanes] * (grad - unit * inner)).astype(BF)
        if pair == 4:
            gain_send(3, gain_sum(2))

    for d in range(1, NX):
        cell_x(d).wait_recv()
    for pair in range(10):
        lanes = slice(pair * 128, pair * 128 + 128)
        if pair < 8:
            cell_k = cell_recv[pair // 2, (pair % 2) * 2]
            cell_v = cell_recv[pair // 2, (pair % 2) * 2 + 1]
        else:
            one = cell_recv[(pair - 8) * 2, 4].astype(F32)
            two = cell_recv[(pair - 8) * 2 + 1, 4].astype(F32)
            cell_k = join(one, two, 0).astype(BF)
            cell_v = join(one, two, 1).astype(BF)
        gv_out[0, :, lanes] = (dot_l(member, cell_v) * 0.25).astype(BF)
        grad = dot_l(member, cell_k) * 0.25 * gain_k
        unit = k_unit[:, lanes]
        inner = head_mean(grad * unit)
        gk_out[0, :, lanes] = (k_scale[:, lanes] * (grad - unit * inner)).astype(BF)

    row = jnp.sum(gain_sum(3), axis=0, keepdims=True)
    row = row + pltpu.roll(row, 64, 1)
    gain_out[...] = jnp.broadcast_to(row / jnp.where(low, gain_q, gain_k), (8, 128))

    for d in range(1, NX):
        kv_x(d).wait_send()
        for part in range(2):
            qg_x(part, d).wait_send()
        for part in range(3):
            out_x(part, d).wait_send()
        cell_x(d).wait_send()
    for part in range(2):
        for s in range(1, 5):
            if on_up(s, part):
                ag_up(s, part).wait_send()
                rs_up(4 - s, part).wait_send()
            if on_down(s, part):
                ag_down(s, part).wait_send()
                rs_down(4 - s, part).wait_send()
        for i in range(8):
            ag_partner(i, 0, part).wait_send()
        for step in range(4):
            core_copy(step, part).wait_send()
    for stage in range(4):
        for copy in gain_copies(stage):
            copy.wait_send()


def local(ny, query_proj, key_proj, value_proj, merge_cells, unmerge, grad_out, query_gain, key_gain):
    vmem = pltpu.VMEM
    dma = pltpu.SemaphoreType.DMA
    block = (5, 128, 128)
    outs = pl.pallas_call(
        functools.partial(kernel, ny),
        out_shape=[jax.ShapeDtypeStruct((1, 128, 1280), BF)] * 4
        + [jax.ShapeDtypeStruct((8, 128), F32)],
        in_specs=[pl.BlockSpec(memory_space=pltpu.VMEM)] * 7,
        out_specs=[pl.BlockSpec(memory_space=pltpu.VMEM)] * 5,
        scratch_shapes=[
            vmem((128, 1280), F32),
            vmem((128, 1280), F32),
            vmem((128, 1280), F32),
            vmem((128, 1280), F32),
            vmem((4, 5, 32, 128), BF),
            vmem((4,) + block, BF),
            vmem((5, 8, 2, 128, 128), BF),
            vmem((4,) + block, BF),
            vmem((5, 512, 128), BF),
            vmem((5, 512, 128), BF),
            vmem((5, 64, 512), BF),
            vmem((5, 64, 512), BF),
            vmem((5, 8, 512, 256), BF),
            vmem((5, 512, 128), F32),
            vmem((5, 512, 128), F32),
            vmem((4, 2, 2) + block, F32),
            vmem((4, 2) + block, BF),
            vmem((4, 2) + block, BF),
            vmem((4,) + block, BF),
            vmem((4,) + block, BF),
            vmem((4,) + block, BF),
            vmem((4,) + block, BF),
            vmem((4,) + block, BF),
            vmem((4,) + block, BF),
            vmem(block, BF),
            vmem((4, 5, 32, 128), BF),
            vmem((4, 8, 128), F32),
            vmem((2, 8, 128), F32),
            vmem((NX, 8, 128), F32),
            vmem((ny, 8, 128), F32),
            vmem((NZ, 8, 128), F32),
            dma((7, 3)),
            dma((7, 3)),
            dma((4, 2)),
            dma((4, 2)),
            dma((4, 2)),
            dma((4, 2)),
            dma((8, 2)),
            dma((8, 2)),
            dma((4, 2)),
            dma((4, 2)),
            dma((4, 2)),
            dma((4, 2)),
            dma((4, 2)),
            dma((4, 2)),
            dma((14,)),
            dma((14,)),
        ],
        compiler_params=pltpu.CompilerParams(
            collective_id=0, has_side_effects=True, vmem_limit_bytes=60 * 1024 * 1024
        ),
        name="attention_block",
    )(
        query_proj,
        key_proj,
        value_proj,
        unmerge,
        grad_out,
        query_gain.reshape(1, 64),
        key_gain.reshape(1, 64),
    )
    return (outs[0], outs[1], outs[2], outs[3], outs[4][0, :64], outs[4][0, 64:])


def solution(mesh):
    placed = (
        P("img", "seq", None),
        P("img", "seq", None),
        P("img", "seq", None),
        P("img", "seq", None),
        P("img", "seq"),
        P("img", "seq", None),
        P(),
        P(),
    )
    return jax.shard_map(
        functools.partial(local, mesh.shape["img"]),
        mesh=mesh,
        in_specs=placed,
        out_specs=(
            P("img", "seq", None),
            P("img", "seq", None),
            P("img", "seq", None),
            P("img", "seq", None),
            P(),
            P(),
        ),
        check_vma=False,
    )
```

```python
import functools

import jax
import jax.numpy as jnp
from jax import lax
from jax.experimental import pallas as pl
from jax.experimental.pallas import tpu as pltpu
from jax.sharding import PartitionSpec as P

BF = jnp.bfloat16
F32 = jnp.float32
EPSILON = 1e-06
NZ, NX = 8, 4
HEADS = ((0, 1, 0, 0), (0, 1, 64, 64), (2, 3, 0, 0), (2, 3, 64, 64), (4, 4, 0, 64))
Q_AT = {0: 0, 2: 1, 4: 2, 1: 3, 3: 4}
PARTS = ((0, 2), (2, 3))


def dot(a, b):
    return jnp.dot(a, b, preferred_element_type=F32)


def dot_t(a, b):
    return lax.dot_general(a, b, (((1,), (1,)), ((), ())), preferred_element_type=F32)


def dot_l(a, b):
    return lax.dot_general(a, b, (((0,), (0,)), ((), ())), preferred_element_type=F32)


def split(value):
    high = value.astype(BF)
    return high, (value - high.astype(F32)).astype(BF)


def kernel(
    ny,
    q_hbm,
    k_hbm,
    v_hbm,
    unmerge_in,
    g_hbm,
    q_gain,
    k_gain,
    att_out,
    gq_out,
    gk_out,
    gv_out,
    gain_out,
    q_unit,
    q_scale,
    k_unit,
    k_scale,
    kv_stage,
    qg_stage,
    kv,
    qg,
    qm,
    gm,
    q_t,
    g_t,
    es,
    acc,
    gq_acc,
    g_all,
    core_send,
    core_recv,
    up_send,
    up_recv,
    dn_send,
    dn_recv,
    out_stage,
    out_recv,
    cell_stage,
    cell_recv,
    gain_own,
    gain_x,
    gain_y,
    gain_z,
    sem_xs,
    sem_xr,
    sem_us,
    sem_ur,
    sem_ds,
    sem_dr,
    sem_ps,
    sem_pr,
    sem_cs,
    sem_cr,
    sem_rus,
    sem_rur,
    sem_rds,
    sem_rdr,
    sem_gs,
    sem_gr,
    sem_in,
    q_in,
    k_in,
    v_in,
    g_in,
):
    img = lax.axis_index("img")
    seq = lax.axis_index("seq")
    core = seq % 2
    x = (seq // 2) % NX
    z = seq // (2 * NX)
    other = 1 - core

    def at(zz, xx, cc):
        return (img, (zz * NX + xx) * 2 + cc)

    up = at((z + 1) % NZ, x, core)
    down = at((z + NZ - 1) % NZ, x, core)
    partner = at(z, x, other)
    x_peers = [at(z, (x + d) % NX, core) for d in range(1, NX)]
    z_peers = [at((z + d) % NZ, x, core) for d in range(1, NZ)]
    y_peers = [((img + d) % ny, seq) for d in range(1, ny)]
    barrier = pltpu.get_barrier_semaphore()
    plane_peers = [partner] + [at(z, (x + d) % NX, c) for d in range(1, NX) for c in (core, other)]
    greeted = plane_peers + z_peers + y_peers
    for device in greeted:
        pl.semaphore_signal(barrier, inc=1, device_id=device, device_id_type=pl.DeviceIdType.MESH)

    def remote(src, dst, send_sem, recv_sem, device):
        return pltpu.make_async_remote_copy(
            src_ref=src,
            dst_ref=dst,
            send_sem=send_sem,
            recv_sem=recv_sem,
            device_id=device,
            device_id_type=pl.DeviceIdType.MESH,
        )

    loads = [
        pltpu.make_async_copy(src, dst, sem_in.at[i])
        for i, (src, dst) in enumerate(((k_hbm, k_in), (v_hbm, v_in), (q_hbm, q_in), (g_hbm, g_in)))
    ]
    for load in loads:
        load.start()
    lane = lax.broadcasted_iota(jnp.int32, (1, 128), 1)
    low = lane < 64
    head_sum = (
        (lax.broadcasted_iota(jnp.int32, (128, 128), 0) < 64)
        == (lax.broadcasted_iota(jnp.int32, (128, 128), 1) < 64)
    ).astype(F32).astype(BF)

    def head_mean(value):
        high, rest = split(value)
        return (dot(high, head_sum) + dot(rest, head_sum)) * (1.0 / 64.0)

    gain_q = jnp.concatenate([q_gain[...], q_gain[...]], axis=1)
    gain_k = jnp.concatenate([k_gain[...], k_gain[...]], axis=1)
    cell = seq * 32 + lax.broadcasted_iota(jnp.int32, (32, 1), 0)
    member = (unmerge_in[...] == cell).astype(F32).astype(BF)

    def pick(first, second, which):
        if which == 0:
            return jnp.where(low, first, pltpu.roll(second, 64, 1)).astype(BF)
        return jnp.where(low, pltpu.roll(first, 64, 1), second).astype(BF)

    loads[0].wait()
    loads[1].wait()
    for pair in range(10):
        lanes = slice(pair * 128, pair * 128 + 128)
        raw = k_in[0, :, lanes].astype(F32)
        scale = lax.rsqrt(head_mean(raw * raw) + EPSILON)
        unit = raw * scale
        k_unit[:, lanes] = unit
        k_scale[:, lanes] = scale
        high, rest = split(unit * gain_k)
        merged_k = (dot(member, high) + dot(member, rest)) * 0.25
        merged_v = dot(member, v_in[0, :, lanes]) * 0.25
        if pair < 8:
            kv_stage[pair // 2, (pair % 2) * 2] = merged_k.astype(BF)
            kv_stage[pair // 2, (pair % 2) * 2 + 1] = merged_v.astype(BF)
        else:
            for which in range(2):
                kv_stage[(pair - 8) * 2 + which, 4] = pick(merged_k, merged_v, which)
    loads[2].wait()
    loads[3].wait()
    for pair in range(10):
        lanes = slice(pair * 128, pair * 128 + 128)
        raw = q_in[0, :, lanes].astype(F32)
        scale = lax.rsqrt(head_mean(raw * raw) + EPSILON)
        unit = raw * scale
        q_unit[:, lanes] = unit
        q_scale[:, lanes] = scale
        normed = (unit * gain_q).astype(BF).astype(F32) * 0.125
        if pair < 8:
            qg_stage[pair // 2, pair % 2] = normed.astype(BF)
        else:
            upstream = g_in[0, :, lanes].astype(F32)
            for which in range(2):
                qg_stage[(pair - 8) * 2 + which, 2] = pick(normed, upstream, which)
    for pair in range(8):
        qg_stage[pair // 2, 3 + pair % 2] = g_in[0, :, pair * 128 : pair * 128 + 128]
    def kv_x(d):
        return remote(
            kv_stage.at[(x + d) % NX],
            kv.at[:, z, core, pl.ds(pl.multiple_of(x * 32, 32), 32), :],
            sem_xs.at[0, d - 1],
            sem_xr.at[0, d - 1],
            x_peers[d - 1],
        )

    def qg_x(part, d):
        blocks = pl.ds(0, 3) if part == 0 else pl.ds(3, 2)
        return remote(
            qg_stage.at[(x + d) % NX, blocks],
            qg.at[x, blocks],
            sem_xs.at[1 + part, d - 1],
            sem_xr.at[1 + part, d - 1],
            x_peers[d - 1],
        )

    pl.semaphore_wait(barrier, len(greeted))

    for d in range(1, NX):
        kv_x(d).start()
    kv[:, z, core, pl.ds(pl.multiple_of(x * 32, 32), 32), :] = kv_stage[x]
    qg[x] = qg_stage[x]

    def z_slot(offset):
        return (z + offset + NZ) % NZ

    def blocks_of(part):
        return pl.ds(*PARTS[part])

    def ag_up(s, part):
        ref = kv.at[blocks_of(part), z_slot(1 - s), core]
        return remote(ref, ref, sem_us.at[s - 1, part], sem_ur.at[s - 1, part], up)

    def ag_down(s, part):
        ref = kv.at[blocks_of(part), z_slot(s - 1), core]
        return remote(ref, ref, sem_ds.at[s - 1, part], sem_dr.at[s - 1, part], down)

    def ag_partner(i, offset, part):
        ref = kv.at[blocks_of(part), z_slot(offset), core]
        return remote(ref, ref, sem_ps.at[i, part], sem_pr.at[i, part], partner)

    def on_up(s, part):
        return s < 4 or part == 0

    def on_down(s, part):
        return s < 4 or part == 1

    def gather_hop(s, part):
        if on_up(s, part):
            ag_up(s, part).wait_recv()
            if s < 4 and on_up(s + 1, part):
                ag_up(s + 1, part).start()
            ag_partner(2 * s - 1, -s, part).start()
        if on_down(s, part):
            ag_down(s, part).wait_recv()
            if s < 4 and on_down(s + 1, part):
                ag_down(s + 1, part).start()
            ag_partner(2 * s if s < 4 else 7, s, part).start()

    for d in range(1, NX):
        kv_x(d).wait_recv()
    for part in range(2):
        ag_up(1, part).start()
        ag_down(1, part).start()
    for d in range(1, NX):
        qg_x(0, d).start()
    for part in range(2):
        ag_partner(0, 0, part).start()

    def head_blocks(h):
        single = (h == 4).astype(jnp.int32)
        base = (h // 2) * 2
        q_block = base
        g_block = base + 1 - single
        q_lane = (h % 2) * 64
        g_lane = q_lane + 64 * single
        return q_block, g_block, pl.multiple_of(q_lane, 64), pl.multiple_of(g_lane, 64)

    def cell_rows(block, first, second):
        return jnp.concatenate(
            [kv[block, first].reshape(256, 128), kv[block, second].reshape(256, 128)], axis=0
        )

    def value_rows(block, g_lane, first, second):
        rows = cell_rows(block, first, second)
        mine = (lane < 64) == (g_lane < 64)
        return jnp.where(mine, rows, jnp.ones_like(rows))

    def forward(first, second, start, stop):
        def body(h, carry):
            q_block, g_block, q_lane, g_lane = head_blocks(h)
            scores = dot_t(qm[h], cell_rows(q_block, first, second))
            weights = jnp.exp(scores).astype(BF)
            es[h, first] = weights[:, :256]
            es[h, second] = weights[:, 256:]
            acc[h] += dot(weights, value_rows(g_block, g_lane, first, second))
            return carry

        lax.fori_loop(start, stop, body, 0)

    def forward_pair(s, start, stop):
        forward(z_slot(-s), z_slot(s - 1), start, stop)

    def wait_partner(indices):
        for i in indices:
            for part in range(2):
                ag_partner(i, 0, part).wait_recv()

    acc[...] = jnp.zeros_like(acc)
    gq_acc[...] = jnp.zeros_like(gq_acc)
    gather_hop(1, 0)
    gather_hop(1, 1)
    for d in range(1, NX):
        qg_x(0, d).wait_recv()
    for h, (q_block, g_block, q_lane, g_lane) in enumerate(HEADS):
        rows = qg[:, Q_AT[q_block]].reshape(512, 128)
        qm[h] = jnp.where(low == (q_lane < 64), rows, jnp.zeros_like(rows))
        if h == 1:
            gather_hop(2, 0)
            for d in range(1, NX):
                qg_x(1, d).start()
    wait_partner((0, 1))
    forward_pair(1, 0, 2)
    gather_hop(2, 1)
    forward_pair(1, 2, 5)
    gather_hop(3, 0)
    wait_partner((2, 3))
    forward_pair(2, 0, 2)
    gather_hop(3, 1)
    forward_pair(2, 2, 5)
    for h, (q_block, g_block, q_lane, g_lane) in enumerate(HEADS):
        q_t[h] = jnp.transpose(qm[h].astype(F32))[q_lane : q_lane + 64].astype(BF)
    wait_partner((4, 5))
    forward_pair(3, 0, 2)
    gather_hop(4, 0)
    forward_pair(3, 2, 5)
    gather_hop(4, 1)
    wait_partner((6, 7))
    forward_pair(4, 0, 5)
    for d in range(1, NX):
        qg_x(1, d).wait_recv()

    attended = []
    for h, (q_block, g_block, q_lane, g_lane) in enumerate(HEADS):
        mine = low == (g_lane < 64)
        total = acc[h]
        inverse = pltpu.roll(1.0 / total, 64, 1)
        weighted = jnp.where(mine, total * inverse, 0.0).astype(BF)
        scaled = jnp.where(mine, qg[:, Q_AT[g_block]].reshape(512, 128).astype(F32) * inverse, 0.0).astype(BF)
        inner = jnp.sum(scaled.astype(F32) * weighted.astype(F32), axis=1, keepdims=True)
        high, rest = split(inner)
        spare = 64 - g_lane
        gm[h] = jnp.where(
            mine,
            scaled,
            jnp.where(lane == spare, -high, jnp.where(lane == spare + 1, -rest, jnp.zeros_like(scaled))),
        )
        g_t[h] = jnp.transpose(scaled.astype(F32))[g_lane : g_lane + 64].astype(BF)
        if h == 0 or h == 2:
            held = weighted
        elif h == 4:
            out_stage[:, 4] = weighted.reshape(4, 128, 128)
        else:
            out_stage[:, h // 2] = jnp.where(low, held, weighted).reshape(4, 128, 128)

    def out_x(part, d):
        blocks = pl.ds(*((0, 2), (2, 1), (3, 2))[part])
        return remote(
            out_stage.at[(x + d) % NX, blocks],
            out_recv.at[x, blocks],
            sem_xs.at[3 + part, d - 1],
            sem_xr.at[3 + part, d - 1],
            x_peers[d - 1],
        )

    for d in range(1, NX):
        out_x(0, d).start()

    def backward(step, first, second, start, stop):
        def body(h, carry):
            q_block, g_block, q_lane, g_lane = head_blocks(h)
            keys = cell_rows(q_block, first, second)
            weights = jnp.concatenate([es[h, first], es[h, second]], axis=1)
            change = dot_t(gm[h], value_rows(g_block, g_lane, first, second))
            grads = (change * weights.astype(F32)).astype(BF)
            gq_acc[h] += dot(grads, keys)
            key_part = dot(q_t[h], grads)
            value_part = dot(g_t[h], weights)
            for i in range(2):
                for c in range(2):
                    cols = slice(i * 256 + c * 128, i * 256 + c * 128 + 128)
                    g_all[step, i, c, q_block, pl.ds(q_lane, 64), :] = key_part[:, cols]
                    g_all[step, i, c, g_block, pl.ds(g_lane, 64), :] = value_part[:, cols]
            return carry

        lax.fori_loop(start, stop, body, 0)

    def core_copy(step, part):
        blocks = blocks_of(part)
        return remote(
            core_send.at[step, :, blocks],
            core_recv.at[step, :, blocks],
            sem_cs.at[step, part],
            sem_cr.at[step, part],
            partner,
        )

    def rs_up(hop, part):
        blocks = blocks_of(part)
        return remote(
            up_send.at[hop, blocks], up_recv.at[hop, blocks], sem_rus.at[hop, part], sem_rur.at[hop, part], up
        )

    def rs_down(hop, part):
        blocks = blocks_of(part)
        return remote(
            dn_send.at[hop, blocks], dn_recv.at[hop, blocks], sem_rds.at[hop, part], sem_rdr.at[hop, part], down
        )

    def chip_sum(step, i, part):
        blocks = blocks_of(part)
        return g_all[step, i, core, blocks] + core_recv[step, i, blocks].astype(F32)

    def send_up(hop, step, i, part):
        value = chip_sum(step, i, part)
        blocks = blocks_of(part)
        if hop > 0 and not (hop == 1 and part == 1):
            rs_up(hop - 1, part).wait_recv()
            value = value + up_recv[hop - 1, blocks].astype(F32)
        up_send[hop, blocks] = value.astype(BF)
        rs_up(hop, part).start()

    def send_down(hop, step, i, part):
        value = chip_sum(step, i, part)
        blocks = blocks_of(part)
        if hop > 0 and not (hop == 1 and part == 0):
            rs_down(hop - 1, part).wait_recv()
            value = value + dn_recv[hop - 1, blocks].astype(F32)
        dn_send[hop, blocks] = value.astype(BF)
        rs_down(hop, part).start()

    def reduce_half(step, part):
        core_copy(step, part).wait_recv()
        if step == 0 and part == 0:
            send_up(0, 0, 0, 0)
        elif step == 0:
            send_down(0, 0, 0, 1)
            send_up(1, 0, 1, 1)
        elif step == 1 and part == 0:
            send_down(1, 1, 0, 0)
            send_up(1, 0, 1, 0)
        elif step < 3:
            if step == 2 and part == 0:
                send_up(2, 1, 1, 0)
            send_down(step, step, 0, part)
            if part == 1:
                send_up(step + 1, step, 1, 1)
        else:
            if part == 0:
                send_up(3, 2, 1, 0)
            send_down(3, 3, 0, part)

    def backward_half(step, part):
        first = z_slot((4, -3, -2, -1)[step])
        second = z_slot((3, 2, 1, 0)[step])
        backward(step, first, second, *((0, 2), (2, 5))[part])
        blocks = blocks_of(part)
        core_send[step, :, blocks] = g_all[step, :, other, blocks].astype(BF)
        core_copy(step, part).start()

    for step in range(4):
        backward_half(step, 0)
        if step > 0:
            reduce_half(step - 1, 1)
        if step == 3:
            out_stage[:, 2] = jnp.where(low, gq_acc[0], gq_acc[1]).astype(BF).reshape(4, 128, 128)
            for d in range(1, NX):
                out_x(1, d).start()
        backward_half(step, 1)
        if step < 3:
            reduce_half(step, 0)

    def gain_copies(stage):
        base, buffer, mine, peers = gain_stages[stage]
        return [
            remote(gain_own.at[stage], buffer.at[mine], sem_gs.at[base + i], sem_gr.at[base + i], device)
            for i, device in enumerate(peers)
        ]

    def gain_send(stage, value):
        base, buffer, mine, peers = gain_stages[stage]
        gain_own[stage] = value
        for copy in gain_copies(stage):
            copy.start()
        buffer[mine] = value

    def gain_sum(stage):
        base, buffer, mine, peers = gain_stages[stage]
        for copy in gain_copies(stage):
            copy.wait_recv()
        result = buffer[0]
        for i in range(1, len(peers) + 1):
            result = result + buffer[i]
        return result

    gain_stages = (
        (0, gain_x, x * 2 + core, plane_peers),
        (7, gain_z, z, z_peers),
        (14, gain_y, img, y_peers),
    )
    tile = jnp.zeros((8, 128), F32)
    for h in range(5):
        tile = tile + jnp.sum((qm[h].astype(F32) * gq_acc[h]).reshape(64, 8, 128), axis=0)
    gain_send(0, tile)
    reduce_half(3, 0)

    out_stage[:, 3] = jnp.where(low, gq_acc[2], gq_acc[3]).astype(BF).reshape(4, 128, 128)
    out_stage[:, 4] = (
        jnp.where(low, gq_acc[4], out_stage[:, 4].reshape(512, 128).astype(F32))
        .astype(BF)
        .reshape(4, 128, 128)
    )
    for d in range(1, NX):
        out_x(2, d).start()
    out_recv[x] = out_stage[x]
    reduce_half(3, 1)

    def join(first, second, which):
        if which == 0:
            return jnp.where(low, first, pltpu.roll(second, 64, 1))
        return jnp.where(low, pltpu.roll(first, 64, 1), second)

    def final_sum():
        for part in range(2):
            rs_up(3, part).wait_recv()
            rs_down(3, part).wait_recv()
        for b in range(5):
            total = (
                g_all[3, 1, core, b]
                + core_recv[3, 1, b].astype(F32)
                + up_recv[3, b].astype(F32)
                + dn_recv[3, b].astype(F32)
            )
            cell_stage[b] = jnp.transpose(total).astype(BF)

    def cell_x(d):
        rows = pl.ds(pl.multiple_of(((x + d) % NX) * 32, 32), 32)
        return remote(
            cell_stage.at[:, rows, :], cell_recv.at[x], sem_xs.at[6, d - 1], sem_xr.at[6, d - 1], x_peers[d - 1]
        )

    for d in range(1, NX):
        out_x(0, d).wait_recv()
    for pair in range(8):
        att_out[0, :, pair * 128 : pair * 128 + 128] = out_recv[pair // 2, pair % 2]
    gain_send(1, gain_sum(0))
    final_sum()
    for d in range(1, NX):
        cell_x(d).start()
    cell_recv[x] = cell_stage[:, pl.ds(pl.multiple_of(x * 32, 32), 32), :]
    gain_send(2, gain_sum(1))

    for part in (1, 2):
        for d in range(1, NX):
            out_x(part, d).wait_recv()
    for pair in range(10):
        lanes = slice(pair * 128, pair * 128 + 128)
        if pair < 8:
            grad = out_recv[pair // 2, 2 + pair % 2].astype(F32)
        else:
            one = out_recv[(pair - 8) * 2, 4].astype(F32)
            two = out_recv[(pair - 8) * 2 + 1, 4].astype(F32)
            att_out[0, :, lanes] = join(one, two, 1).astype(BF)
            grad = join(one, two, 0)
        grad = grad * 0.125 * gain_q
        unit = q_unit[:, lanes]
        inner = head_mean(grad * unit)
        gq_out[0, :, lanes] = (q_scale[:, lanes] * (grad - unit * inner)).astype(BF)

    for d in range(1, NX):
        cell_x(d).wait_recv()
    for pair in range(10):
        lanes = slice(pair * 128, pair * 128 + 128)
        if pair < 8:
            cell_k = cell_recv[pair // 2, (pair % 2) * 2]
            cell_v = cell_recv[pair // 2, (pair % 2) * 2 + 1]
        else:
            one = cell_recv[(pair - 8) * 2, 4].astype(F32)
            two = cell_recv[(pair - 8) * 2 + 1, 4].astype(F32)
            cell_k = join(one, two, 0).astype(BF)
            cell_v = join(one, two, 1).astype(BF)
        gv_out[0, :, lanes] = (dot_l(member, cell_v) * 0.25).astype(BF)
        grad = dot_l(member, cell_k) * 0.25 * gain_k
        unit = k_unit[:, lanes]
        inner = head_mean(grad * unit)
        gk_out[0, :, lanes] = (k_scale[:, lanes] * (grad - unit * inner)).astype(BF)

    row = jnp.sum(gain_sum(2), axis=0, keepdims=True)
    row = row + pltpu.roll(row, 64, 1)
    gain_out[...] = jnp.broadcast_to(row / jnp.where(low, gain_q, gain_k), (8, 128))

    for d in range(1, NX):
        kv_x(d).wait_send()
        for part in range(2):
            qg_x(part, d).wait_send()
        for part in range(3):
            out_x(part, d).wait_send()
        cell_x(d).wait_send()
    for part in range(2):
        for s in range(1, 5):
            if on_up(s, part):
                ag_up(s, part).wait_send()
                rs_up(4 - s, part).wait_send()
            if on_down(s, part):
                ag_down(s, part).wait_send()
                rs_down(4 - s, part).wait_send()
        for i in range(8):
            ag_partner(i, 0, part).wait_send()
        for step in range(4):
            core_copy(step, part).wait_send()
    for stage in range(3):
        for copy in gain_copies(stage):
            copy.wait_send()


def finish(att, gq, gk, gv, gain, att_out, gq_out, gk_out, gv_out, q_gain_out, k_gain_out):
    att_out[...] = att[...]
    gq_out[...] = gq[...]
    gk_out[...] = gk[...]
    gv_out[...] = gv[...]
    q_gain_out[...] = gain[0:1, :64]
    k_gain_out[...] = pltpu.roll(gain[...], 64, 1)[0:1, :64]


def local(ny, query_proj, key_proj, value_proj, merge_cells, unmerge, grad_out, query_gain, key_gain):
    vmem = pltpu.VMEM
    dma = pltpu.SemaphoreType.DMA
    block = (5, 128, 128)
    outs = pl.pallas_call(
        functools.partial(kernel, ny),
        out_shape=[jax.ShapeDtypeStruct((1, 128, 1280), BF)] * 4
        + [jax.ShapeDtypeStruct((8, 128), F32)],
        in_specs=[pl.BlockSpec(memory_space=pl.ANY)] * 3
        + [pl.BlockSpec(memory_space=pltpu.VMEM), pl.BlockSpec(memory_space=pl.ANY)]
        + [pl.BlockSpec(memory_space=pltpu.VMEM)] * 2,
        out_specs=[pl.BlockSpec(memory_space=pltpu.VMEM)] * 5,
        scratch_shapes=[
            vmem((128, 1280), F32),
            vmem((128, 1280), F32),
            vmem((128, 1280), F32),
            vmem((128, 1280), F32),
            vmem((4, 5, 32, 128), BF),
            vmem((4,) + block, BF),
            vmem((5, 8, 2, 128, 128), BF),
            vmem((4,) + block, BF),
            vmem((5, 512, 128), BF),
            vmem((5, 512, 128), BF),
            vmem((5, 64, 512), BF),
            vmem((5, 64, 512), BF),
            vmem((5, 8, 512, 256), BF),
            vmem((5, 512, 128), F32),
            vmem((5, 512, 128), F32),
            vmem((4, 2, 2) + block, F32),
            vmem((4, 2) + block, BF),
            vmem((4, 2) + block, BF),
            vmem((4,) + block, BF),
            vmem((4,) + block, BF),
            vmem((4,) + block, BF),
            vmem((4,) + block, BF),
            vmem((4,) + block, BF),
            vmem((4,) + block, BF),
            vmem(block, BF),
            vmem((4, 5, 32, 128), BF),
            vmem((4, 8, 128), F32),
            vmem((2 * NX, 8, 128), F32),
            vmem((ny, 8, 128), F32),
            vmem((NZ, 8, 128), F32),
            dma((7, 3)),
            dma((7, 3)),
            dma((4, 2)),
            dma((4, 2)),
            dma((4, 2)),
            dma((4, 2)),
            dma((8, 2)),
            dma((8, 2)),
            dma((4, 2)),
            dma((4, 2)),
            dma((4, 2)),
            dma((4, 2)),
            dma((4, 2)),
            dma((4, 2)),
            dma((17,)),
            dma((17,)),
            dma((4,)),
            vmem((1, 128, 1280), BF),
            vmem((1, 128, 1280), BF),
            vmem((1, 128, 1280), BF),
            vmem((1, 128, 1280), BF),
        ],
        compiler_params=pltpu.CompilerParams(
            collective_id=0, has_side_effects=True, vmem_limit_bytes=60 * 1024 * 1024
        ),
        name="attention_block",
    )(
        query_proj,
        key_proj,
        value_proj,
        unmerge,
        grad_out,
        query_gain.reshape(1, 64),
        key_gain.reshape(1, 64),
    )
    done = pl.pallas_call(
        finish,
        out_shape=[jax.ShapeDtypeStruct((1, 128, 1280), BF)] * 4 + [jax.ShapeDtypeStruct((1, 64), F32)] * 2,
        in_specs=[pl.BlockSpec(memory_space=pltpu.VMEM)] * 5,
        out_specs=[pl.BlockSpec(memory_space=pltpu.VMEM)] * 6,
        name="finish",
    )(*outs)
    return (*done[:4], done[4].reshape(64), done[5].reshape(64))


def solution(mesh):
    placed = (
        P("img", "seq", None),
        P("img", "seq", None),
        P("img", "seq", None),
        P("img", "seq", None),
        P("img", "seq"),
        P("img", "seq", None),
        P(),
        P(),
    )
    return jax.shard_map(
        functools.partial(local, mesh.shape["img"]),
        mesh=mesh,
        in_specs=placed,
        out_specs=(
            P("img", "seq", None),
            P("img", "seq", None),
            P("img", "seq", None),
            P("img", "seq", None),
            P(),
            P(),
        ),
        check_vma=False,
    )
```

```python
import functools

import jax
import jax.numpy as jnp
from jax import lax
from jax.experimental import pallas as pl
from jax.experimental.pallas import tpu as pltpu
from jax.sharding import PartitionSpec as P

BF = jnp.bfloat16
F32 = jnp.float32
EPSILON = 1e-06
NZ, NX = 8, 4
HEADS = ((0, 1, 0, 0), (0, 1, 64, 64), (2, 3, 0, 0), (2, 3, 64, 64), (4, 4, 0, 64))
Q_AT = {0: 0, 2: 1, 4: 2, 1: 3, 3: 4}
PARTS = ((0, 2), (2, 2), (4, 1))
PART_HEADS = ((0, 2), (2, 4), (4, 5))


def dot(a, b):
    return jnp.dot(a, b, preferred_element_type=F32)


def dot_t(a, b):
    return lax.dot_general(a, b, (((1,), (1,)), ((), ())), preferred_element_type=F32)


def dot_l(a, b):
    return lax.dot_general(a, b, (((0,), (0,)), ((), ())), preferred_element_type=F32)


def split(value):
    high = value.astype(BF)
    return high, (value - high.astype(F32)).astype(BF)


def kernel(
    ny,
    q_hbm,
    k_hbm,
    v_hbm,
    unmerge_in,
    g_hbm,
    q_gain,
    k_gain,
    att_out,
    gq_out,
    gk_out,
    gv_out,
    gain_out,
    q_unit,
    q_scale,
    k_unit,
    k_scale,
    kv_stage,
    qg_stage,
    kv,
    qg,
    qm,
    gm,
    q_t,
    g_t,
    es,
    acc,
    gq_acc,
    g_all,
    core_send,
    core_recv,
    up_send,
    up_recv,
    dn_send,
    dn_recv,
    out_stage,
    out_recv,
    cell_stage,
    cell_recv,
    gain_own,
    gain_x,
    gain_z,
    sem_xs,
    sem_xr,
    sem_us,
    sem_ur,
    sem_ds,
    sem_dr,
    sem_ps,
    sem_pr,
    sem_cs,
    sem_cr,
    sem_rus,
    sem_rur,
    sem_rds,
    sem_rdr,
    sem_gs,
    sem_gr,
    sem_fs,
    sem_fr,
    sem_in,
    q_in,
    k_in,
    v_in,
    g_in,
):
    img = lax.axis_index("img")
    seq = lax.axis_index("seq")
    core = seq % 2
    x = (seq // 2) % NX
    z = seq // (2 * NX)
    other = 1 - core

    def at(zz, xx, cc):
        return (img, (zz * NX + xx) * 2 + cc)

    sign = 1 - 2 * core
    onward = at((z + sign + NZ) % NZ, x, core)
    up = at((z + 1) % NZ, x, core)
    down = at((z + NZ - 1) % NZ, x, core)
    partner = at(z, x, other)
    x_peers = [at(z, (x + d) % NX, core) for d in range(1, NX)]
    z_peers = [at((z + d) % NZ, x, core) for d in range(1, NZ)]
    barrier = pltpu.get_barrier_semaphore()
    plane_peers = [partner] + [at(z, (x + d) % NX, c) for d in range(1, NX) for c in (core, other)]
    for e in range(1, ny):
        for d in range(NX):
            for c in (core, other):
                plane_peers.append(((img + e) % ny, (z * NX + (x + d) % NX) * 2 + c))
    greeted = plane_peers + z_peers
    for device in greeted:
        pl.semaphore_signal(barrier, inc=1, device_id=device, device_id_type=pl.DeviceIdType.MESH)

    def remote(src, dst, send_sem, recv_sem, device):
        return pltpu.make_async_remote_copy(
            src_ref=src,
            dst_ref=dst,
            send_sem=send_sem,
            recv_sem=recv_sem,
            device_id=device,
            device_id_type=pl.DeviceIdType.MESH,
        )

    loads = [
        pltpu.make_async_copy(src, dst, sem_in.at[i])
        for i, (src, dst) in enumerate(((k_hbm, k_in), (v_hbm, v_in), (q_hbm, q_in), (g_hbm, g_in)))
    ]
    loads[0].start()
    loads[1].start()
    lane = lax.broadcasted_iota(jnp.int32, (1, 128), 1)
    low = lane < 64
    head_sum = (
        (lax.broadcasted_iota(jnp.int32, (128, 128), 0) < 64)
        == (lax.broadcasted_iota(jnp.int32, (128, 128), 1) < 64)
    ).astype(F32).astype(BF)

    head_sum2 = jnp.concatenate([head_sum, head_sum], axis=0)

    def head_mean(value):
        return dot(jnp.concatenate(split(value), axis=1), head_sum2) * (1.0 / 64.0)

    gain_q = jnp.concatenate([q_gain[...], q_gain[...]], axis=1)
    gain_k = jnp.concatenate([k_gain[...], k_gain[...]], axis=1)
    cell = seq * 32 + lax.broadcasted_iota(jnp.int32, (32, 1), 0)
    member = (unmerge_in[...] == cell).astype(F32).astype(BF)

    def pick(first, second, which):
        if which == 0:
            return jnp.where(low, first, pltpu.roll(second, 64, 1)).astype(BF)
        return jnp.where(low, pltpu.roll(first, 64, 1), second).astype(BF)

    member2 = jnp.concatenate([member, member], axis=1)
    loads[0].wait()
    loads[2].start()
    loads[3].start()
    merged_k = []
    for two in range(5):
        normed = []
        for pair in (2 * two, 2 * two + 1):
            lanes = slice(pair * 128, pair * 128 + 128)
            raw = k_in[0, :, lanes].astype(F32)
            scale = lax.rsqrt(head_mean(raw * raw) + EPSILON)
            unit = raw * scale
            k_unit[:, lanes] = unit
            k_scale[:, lanes] = scale
            normed.append(unit * gain_k)
        rows = jnp.concatenate(split(jnp.concatenate(normed, axis=1)), axis=0)
        merged_k.append(dot(member2, rows) * 0.25)
    loads[1].wait()
    for two in range(5):
        merged_v = dot(member, v_in[0, :, two * 256 : two * 256 + 256]) * 0.25
        for i in range(2):
            one_k, one_v = merged_k[two][:, i * 128 : i * 128 + 128], merged_v[:, i * 128 : i * 128 + 128]
            if two < 4:
                kv_stage[two, 2 * i] = one_k.astype(BF)
                kv_stage[two, 2 * i + 1] = one_v.astype(BF)
            else:
                for which in range(2):
                    kv_stage[2 * i + which, 4] = pick(one_k, one_v, which)
    loads[2].wait()
    loads[3].wait()
    for pair in range(10):
        lanes = slice(pair * 128, pair * 128 + 128)
        raw = q_in[0, :, lanes].astype(F32)
        scale = lax.rsqrt(head_mean(raw * raw) + EPSILON)
        unit = raw * scale
        q_unit[:, lanes] = unit
        q_scale[:, lanes] = scale
        normed = (unit * gain_q).astype(BF).astype(F32) * 0.125
        if pair < 8:
            qg_stage[pair // 2, pair % 2] = normed.astype(BF)
        else:
            upstream = g_in[0, :, lanes].astype(F32)
            for which in range(2):
                qg_stage[(pair - 8) * 2 + which, 2] = pick(normed, upstream, which)
    for pair in range(8):
        qg_stage[pair // 2, 3 + pair % 2] = g_in[0, :, pair * 128 : pair * 128 + 128]
    def kv_x(d):
        return remote(
            kv_stage.at[(x + d) % NX],
            kv.at[:, z, core, pl.ds(pl.multiple_of(x * 32, 32), 32), :],
            sem_xs.at[0, d - 1],
            sem_xr.at[0, d - 1],
            x_peers[d - 1],
        )

    def qg_x(part, d):
        blocks = pl.ds(0, 3) if part == 0 else pl.ds(3, 2)
        return remote(
            qg_stage.at[(x + d) % NX, blocks],
            qg.at[x, blocks],
            sem_xs.at[1 + part, d - 1],
            sem_xr.at[1 + part, d - 1],
            x_peers[d - 1],
        )

    pl.semaphore_wait(barrier, len(greeted))

    for d in range(1, NX):
        kv_x(d).start()
    kv[:, z, core, pl.ds(pl.multiple_of(x * 32, 32), 32), :] = kv_stage[x]
    qg[x] = qg_stage[x]

    def z_slot(offset):
        return (z + offset + NZ) % NZ

    def blocks_of(part):
        return pl.ds(*PARTS[part])

    def far(s):
        return z_slot(-sign * s)

    def half(part):
        return core if part == 0 else other

    def ag_ring(s, part):
        ref = kv.at[:, far(s - 1), half(part)]
        return remote(ref, ref, sem_us.at[s - 1, part], sem_ur.at[s - 1, part], onward)

    def ag_partner(s, part):
        ref = kv.at[:, far(s), half(part)]
        return remote(ref, ref, sem_ps.at[s, part], sem_pr.at[s, part], partner)

    def piece(index, d):
        return kv.at[:, z, index, pl.ds(pl.multiple_of(((x + NX - d) % NX) * 32, 32), 32), :]

    def first_ring(part, d):
        ref = piece(half(part), d)
        return remote(ref, ref, sem_fs.at[part, d], sem_fr.at[part, d], onward)

    def first_partner(d):
        ref = piece(core, d)
        return remote(ref, ref, sem_fs.at[2, d], sem_fr.at[2, d], partner)

    def gather_hop(s, part):
        if s == 1:
            for d in range(NX):
                first_ring(part, d).wait_recv()
        else:
            ag_ring(s, part).wait_recv()
        if s < 3 or (s == 3 and part == 0):
            ag_ring(s + 1, part).start()
        ag_partner(s, part).start()

    for d in (0, 1, 3, 2):
        if d > 0:
            kv_x(d).wait_recv()
        first_ring(0, d).start()
        first_partner(d).start()
    for d in range(1, NX):
        qg_x(0, d).start()
    for d in (0, 1, 3, 2):
        first_partner(d).wait_recv()
        first_ring(1, d).start()

    def head_blocks(h):
        single = (h == 4).astype(jnp.int32)
        base = (h // 2) * 2
        q_block = base
        g_block = base + 1 - single
        q_lane = (h % 2) * 64
        g_lane = q_lane + 64 * single
        return q_block, g_block, pl.multiple_of(q_lane, 64), pl.multiple_of(g_lane, 64)

    def cell_rows(block, first, second):
        return jnp.concatenate(
            [kv[block, first].reshape(256, 128), kv[block, second].reshape(256, 128)], axis=0
        )

    def value_rows(block, g_lane, first, second):
        rows = cell_rows(block, first, second)
        mine = (lane < 64) == (g_lane < 64)
        return jnp.where(mine, rows, jnp.ones_like(rows))

    def forward(first, second, start, stop):
        def body(h, carry):
            q_block, g_block, q_lane, g_lane = head_blocks(h)
            scores = dot_t(qm[h], cell_rows(q_block, first, second))
            weights = jnp.exp(scores).astype(BF)
            es[h, first] = weights[:, :256]
            es[h, second] = weights[:, 256:]
            acc[h] += dot(weights, value_rows(g_block, g_lane, first, second))
            return carry

        lax.fori_loop(start, stop, body, 0)

    def forward_pair(s, start, stop):
        forward(far(s), far(1 - s), start, stop)

    def wait_partner(s):
        for part in range(2 if s < 4 else 1):
            ag_partner(s, part).wait_recv()

    acc[...] = jnp.zeros_like(acc)
    gq_acc[...] = jnp.zeros_like(gq_acc)
    gather_hop(1, 0)
    gather_hop(1, 1)
    for d in range(1, NX):
        qg_x(0, d).wait_recv()
    for h, (q_block, g_block, q_lane, g_lane) in enumerate(HEADS):
        rows = qg[:, Q_AT[q_block]].reshape(512, 128)
        qm[h] = jnp.where(low == (q_lane < 64), rows, jnp.zeros_like(rows))
        if h == 1:
            gather_hop(2, 0)
            for d in range(1, NX):
                qg_x(1, d).start()
    forward_pair(1, 0, 2)
    gather_hop(2, 1)
    forward_pair(1, 2, 5)
    gather_hop(3, 0)
    wait_partner(1)
    forward_pair(2, 0, 2)
    gather_hop(3, 1)
    forward_pair(2, 2, 5)
    for h, (q_block, g_block, q_lane, g_lane) in enumerate(HEADS):
        q_t[h] = jnp.transpose(qm[h].astype(F32))[q_lane : q_lane + 64].astype(BF)
    wait_partner(2)
    forward_pair(3, 0, 2)
    gather_hop(4, 0)
    forward_pair(3, 2, 5)
    wait_partner(3)
    wait_partner(4)
    def finish_head(h):
        q_block, g_block, q_lane, g_lane = HEADS[h]
        mine = low == (g_lane < 64)
        total = acc[h]
        inverse = pltpu.roll(1.0 / total, 64, 1)
        weighted = jnp.where(mine, total * inverse, 0.0).astype(BF)
        scaled = jnp.where(mine, qg[:, Q_AT[g_block]].reshape(512, 128).astype(F32) * inverse, 0.0).astype(BF)
        inner = jnp.sum(scaled.astype(F32) * weighted.astype(F32), axis=1, keepdims=True)
        high, rest = split(inner)
        spare = 64 - g_lane
        gm[h] = jnp.where(
            mine,
            scaled,
            jnp.where(lane == spare, -high, jnp.where(lane == spare + 1, -rest, jnp.zeros_like(scaled))),
        )
        g_t[h] = jnp.transpose(scaled.astype(F32))[g_lane : g_lane + 64].astype(BF)
        return weighted

    def finalize(part):
        if part == 0:
            pairs = (0,)
        else:
            pairs = (1,)
            out_stage[:, 4] = finish_head(4).reshape(4, 128, 128)
        for pair in pairs:
            first, second = finish_head(2 * pair), finish_head(2 * pair + 1)
            out_stage[:, pair] = jnp.where(low, first, second).reshape(4, 128, 128)

    def out_x(part, d):
        blocks = pl.ds(*((0, 2), (2, 1), (3, 2))[part])
        return remote(
            out_stage.at[(x + d) % NX, blocks],
            out_recv.at[x, blocks],
            sem_xs.at[3 + part, d - 1],
            sem_xr.at[3 + part, d - 1],
            x_peers[d - 1],
        )

    def backward(step, first, second, start, stop):
        def body(h, carry):
            q_block, g_block, q_lane, g_lane = head_blocks(h)
            keys = cell_rows(q_block, first, second)
            weights = jnp.concatenate([es[h, first], es[h, second]], axis=1)
            change = dot_t(gm[h], value_rows(g_block, g_lane, first, second))
            grads = (change * weights.astype(F32)).astype(BF)
            gq_acc[h] += dot(grads, keys)
            key_part = dot(q_t[h], grads)
            value_part = dot(g_t[h], weights)
            for i in range(2):
                for c in range(2):
                    cols = slice(i * 256 + c * 128, i * 256 + c * 128 + 128)
                    g_all[step, i, c, q_block, pl.ds(q_lane, 64), :] = key_part[:, cols]
                    g_all[step, i, c, g_block, pl.ds(g_lane, 64), :] = value_part[:, cols]
            return carry

        lax.fori_loop(start, stop, body, 0)

    def core_copy(step, part):
        blocks = blocks_of(part)
        return remote(
            core_send.at[step, :, blocks],
            core_recv.at[step, :, blocks],
            sem_cs.at[step, part],
            sem_cr.at[step, part],
            partner,
        )

    def rs_up(hop, part):
        blocks = blocks_of(part)
        return remote(
            up_send.at[hop, blocks], up_recv.at[hop, blocks], sem_rus.at[hop, part], sem_rur.at[hop, part], up
        )

    def rs_down(hop, part):
        blocks = blocks_of(part)
        return remote(
            dn_send.at[hop, blocks], dn_recv.at[hop, blocks], sem_rds.at[hop, part], sem_rdr.at[hop, part], down
        )

    def chip_sum(step, i, part):
        blocks = blocks_of(part)
        return g_all[step, i, core, blocks] + core_recv[step, i, blocks].astype(F32)

    def send_up(hop, step, i, part):
        value = chip_sum(step, i, part)
        blocks = blocks_of(part)
        if hop > 0 and not (hop == 1 and part > 0):
            rs_up(hop - 1, part).wait_recv()
            value = value + up_recv[hop - 1, blocks].astype(F32)
        up_send[hop, blocks] = value.astype(BF)
        rs_up(hop, part).start()

    def send_down(hop, step, i, part):
        value = chip_sum(step, i, part)
        blocks = blocks_of(part)
        if hop > 0 and not (hop == 1 and part == 0):
            rs_down(hop - 1, part).wait_recv()
            value = value + dn_recv[hop - 1, blocks].astype(F32)
        dn_send[hop, blocks] = value.astype(BF)
        rs_down(hop, part).start()

    def reduce_half(step, part):
        core_copy(step, part).wait_recv()
        if step == 0 and part == 0:
            send_up(0, 0, 0, 0)
        elif step == 0:
            send_down(0, 0, 0, part)
            send_up(1, 0, 1, part)
        elif step == 1 and part == 0:
            send_down(1, 1, 0, 0)
            send_up(1, 0, 1, 0)
        elif step < 3:
            if step == 2 and part == 0:
                send_up(2, 1, 1, 0)
            send_down(step, step, 0, part)
            if part > 0:
                send_up(step + 1, step, 1, part)
        else:
            if part == 0:
                send_up(3, 2, 1, 0)
            send_down(3, 3, 0, part)

    def backward_half(step, part):
        first = z_slot((4, -3, -2, -1)[step])
        second = z_slot((3, 2, 1, 0)[step])
        backward(step, first, second, *PART_HEADS[part])
        blocks = blocks_of(part)
        core_send[step, :, blocks] = g_all[step, :, other, blocks].astype(BF)
        core_copy(step, part).start()

    forward_pair(4, 0, 2)
    for d in range(1, NX):
        qg_x(1, d).wait_recv()
    finalize(0)
    backward_half(0, 0)
    forward_pair(4, 2, 5)
    finalize(1)
    for d in range(1, NX):
        out_x(0, d).start()
    reduce_half(0, 0)
    backward_half(0, 1)
    backward_half(0, 2)
    backward_half(1, 0)
    reduce_half(0, 1)
    reduce_half(0, 2)
    backward_half(1, 1)
    backward_half(1, 2)
    reduce_half(1, 0)
    backward_half(2, 0)
    reduce_half(1, 1)
    reduce_half(1, 2)
    backward_half(2, 1)
    backward_half(2, 2)
    reduce_half(2, 0)
    backward_half(3, 0)
    out_stage[:, 2] = jnp.where(low, gq_acc[0], gq_acc[1]).astype(BF).reshape(4, 128, 128)
    for d in range(1, NX):
        out_x(1, d).start()
    reduce_half(2, 1)
    reduce_half(2, 2)
    backward_half(3, 1)
    backward_half(3, 2)

    def gain_copies(stage):
        base, buffer, mine, peers = gain_stages[stage]
        return [
            remote(gain_own.at[stage], buffer.at[mine], sem_gs.at[base + i], sem_gr.at[base + i], device)
            for i, device in enumerate(peers)
        ]

    def gain_send(stage, value):
        base, buffer, mine, peers = gain_stages[stage]
        gain_own[stage] = value
        for copy in gain_copies(stage):
            copy.start()
        buffer[mine] = value

    def gain_sum(stage):
        base, buffer, mine, peers = gain_stages[stage]
        for copy in gain_copies(stage):
            copy.wait_recv()
        result = buffer[0]
        for i in range(1, len(peers) + 1):
            result = result + buffer[i]
        return result

    gain_stages = (
        (0, gain_x, (img * NX + x) * 2 + core, plane_peers),
        (len(plane_peers), gain_z, z, z_peers),
    )
    tile = jnp.zeros((8, 128), F32)
    for h in range(5):
        tile = tile + jnp.sum((qm[h].astype(F32) * gq_acc[h]).reshape(64, 8, 128), axis=0)
    gain_send(0, jnp.sum(tile, axis=0, keepdims=True))
    reduce_half(3, 0)

    out_stage[:, 3] = jnp.where(low, gq_acc[2], gq_acc[3]).astype(BF).reshape(4, 128, 128)
    out_stage[:, 4] = (
        jnp.where(low, gq_acc[4], out_stage[:, 4].reshape(512, 128).astype(F32))
        .astype(BF)
        .reshape(4, 128, 128)
    )
    for d in range(1, NX):
        out_x(2, d).start()
    out_recv[x] = out_stage[x]
    reduce_half(3, 1)
    reduce_half(3, 2)

    def join(first, second, which):
        if which == 0:
            return jnp.where(low, first, pltpu.roll(second, 64, 1))
        return jnp.where(low, pltpu.roll(first, 64, 1), second)

    def final_sum():
        for part in range(3):
            rs_up(3, part).wait_recv()
            rs_down(3, part).wait_recv()
        for b in range(5):
            total = (
                g_all[3, 1, core, b]
                + core_recv[3, 1, b].astype(F32)
                + up_recv[3, b].astype(F32)
                + dn_recv[3, b].astype(F32)
            )
            cell_stage[b] = jnp.transpose(total).astype(BF)

    def cell_x(d):
        rows = pl.ds(pl.multiple_of(((x + d) % NX) * 32, 32), 32)
        return remote(
            cell_stage.at[:, rows, :], cell_recv.at[x], sem_xs.at[6, d - 1], sem_xr.at[6, d - 1], x_peers[d - 1]
        )

    for d in range(1, NX):
        out_x(0, d).wait_recv()
    for pair in range(8):
        att_out[0, :, pair * 128 : pair * 128 + 128] = out_recv[pair // 2, pair % 2]
    final_sum()
    for d in range(1, NX):
        cell_x(d).start()
    cell_recv[x] = cell_stage[:, pl.ds(pl.multiple_of(x * 32, 32), 32), :]
    gain_send(1, gain_sum(0))

    for part in (1, 2):
        for d in range(1, NX):
            out_x(part, d).wait_recv()
    for pair in range(10):
        lanes = slice(pair * 128, pair * 128 + 128)
        if pair < 8:
            grad = out_recv[pair // 2, 2 + pair % 2].astype(F32)
        else:
            one = out_recv[(pair - 8) * 2, 4].astype(F32)
            two = out_recv[(pair - 8) * 2 + 1, 4].astype(F32)
            att_out[0, :, lanes] = join(one, two, 1).astype(BF)
            grad = join(one, two, 0)
        grad = grad * 0.125 * gain_q
        unit = q_unit[:, lanes]
        inner = head_mean(grad * unit)
        gq_out[0, :, lanes] = (q_scale[:, lanes] * (grad - unit * inner)).astype(BF)

    for d in range(1, NX):
        cell_x(d).wait_recv()
    for pair in range(10):
        lanes = slice(pair * 128, pair * 128 + 128)
        if pair < 8:
            cell_k = cell_recv[pair // 2, (pair % 2) * 2]
            cell_v = cell_recv[pair // 2, (pair % 2) * 2 + 1]
        else:
            one = cell_recv[(pair - 8) * 2, 4].astype(F32)
            two = cell_recv[(pair - 8) * 2 + 1, 4].astype(F32)
            cell_k = join(one, two, 0).astype(BF)
            cell_v = join(one, two, 1).astype(BF)
        gv_out[0, :, lanes] = (dot_l(member, cell_v) * 0.25).astype(BF)
        grad = dot_l(member, cell_k) * 0.25 * gain_k
        unit = k_unit[:, lanes]
        inner = head_mean(grad * unit)
        gk_out[0, :, lanes] = (k_scale[:, lanes] * (grad - unit * inner)).astype(BF)

    row = gain_sum(1)
    row = row + pltpu.roll(row, 64, 1)
    gain_out[...] = jnp.broadcast_to(row / jnp.where(low, gain_q, gain_k), (8, 128))

    for d in range(1, NX):
        kv_x(d).wait_send()
        for part in range(2):
            qg_x(part, d).wait_send()
        for part in range(3):
            out_x(part, d).wait_send()
        cell_x(d).wait_send()
    for d in range(NX):
        first_partner(d).wait_send()
        for part in range(2):
            first_ring(part, d).wait_send()
    for s in range(1, 5):
        for part in range(2):
            if s < 4 or part == 0:
                if s > 1:
                    ag_ring(s, part).wait_send()
                ag_partner(s, part).wait_send()
    for step in range(4):
        for part in range(3):
            core_copy(step, part).wait_send()
            if step > 0 or part == 0:
                rs_up(step, part).wait_send()
            if step > 0 or part > 0:
                rs_down(step, part).wait_send()
    for stage in range(2):
        for copy in gain_copies(stage):
            copy.wait_send()


def finish(att, gq, gk, gv, gain, att_out, gq_out, gk_out, gv_out, q_gain_out, k_gain_out):
    att_out[...] = att[...]
    gq_out[...] = gq[...]
    gk_out[...] = gk[...]
    gv_out[...] = gv[...]
    q_gain_out[...] = gain[0:1, :64]
    k_gain_out[...] = pltpu.roll(gain[...], 64, 1)[0:1, :64]


def local(ny, query_proj, key_proj, value_proj, merge_cells, unmerge, grad_out, query_gain, key_gain):
    vmem = pltpu.VMEM
    dma = pltpu.SemaphoreType.DMA
    block = (5, 128, 128)
    outs = pl.pallas_call(
        functools.partial(kernel, ny),
        out_shape=[jax.ShapeDtypeStruct((1, 128, 1280), BF)] * 4
        + [jax.ShapeDtypeStruct((8, 128), F32)],
        in_specs=[pl.BlockSpec(memory_space=pl.ANY)] * 3
        + [pl.BlockSpec(memory_space=pltpu.VMEM), pl.BlockSpec(memory_space=pl.ANY)]
        + [pl.BlockSpec(memory_space=pltpu.VMEM)] * 2,
        out_specs=[pl.BlockSpec(memory_space=pltpu.VMEM)] * 5,
        scratch_shapes=[
            vmem((128, 1280), F32),
            vmem((128, 1280), F32),
            vmem((128, 1280), F32),
            vmem((128, 1280), F32),
            vmem((4, 5, 32, 128), BF),
            vmem((4,) + block, BF),
            vmem((5, 8, 2, 128, 128), BF),
            vmem((4,) + block, BF),
            vmem((5, 512, 128), BF),
            vmem((5, 512, 128), BF),
            vmem((5, 64, 512), BF),
            vmem((5, 64, 512), BF),
            vmem((5, 8, 512, 256), BF),
            vmem((5, 512, 128), F32),
            vmem((5, 512, 128), F32),
            vmem((4, 2, 2) + block, F32),
            vmem((4, 2) + block, BF),
            vmem((4, 2) + block, BF),
            vmem((4,) + block, BF),
            vmem((4,) + block, BF),
            vmem((4,) + block, BF),
            vmem((4,) + block, BF),
            vmem((4,) + block, BF),
            vmem((4,) + block, BF),
            vmem(block, BF),
            vmem((4, 5, 32, 128), BF),
            vmem((2, 1, 128), F32),
            vmem((2 * NX * ny, 1, 128), F32),
            vmem((NZ, 1, 128), F32),
            dma((7, 3)),
            dma((7, 3)),
            dma((4, 3)),
            dma((4, 3)),
            dma((4, 3)),
            dma((4, 3)),
            dma((8, 2)),
            dma((8, 2)),
            dma((4, 3)),
            dma((4, 3)),
            dma((4, 3)),
            dma((4, 3)),
            dma((4, 3)),
            dma((4, 3)),
            dma((2 * NX * ny - 1 + NZ - 1,)),
            dma((2 * NX * ny - 1 + NZ - 1,)),
            dma((3, 4)),
            dma((3, 4)),
            dma((4,)),
            vmem((1, 128, 1280), BF),
            vmem((1, 128, 1280), BF),
            vmem((1, 128, 1280), BF),
            vmem((1, 128, 1280), BF),
        ],
        compiler_params=pltpu.CompilerParams(
            collective_id=0, has_side_effects=True, vmem_limit_bytes=60 * 1024 * 1024
        ),
        name="attention_block",
    )(
        query_proj,
        key_proj,
        value_proj,
        unmerge,
        grad_out,
        query_gain.reshape(1, 64),
        key_gain.reshape(1, 64),
    )
    done = pl.pallas_call(
        finish,
        out_shape=[jax.ShapeDtypeStruct((1, 128, 1280), BF)] * 4 + [jax.ShapeDtypeStruct((1, 64), F32)] * 2,
        in_specs=[pl.BlockSpec(memory_space=pltpu.VMEM)] * 5,
        out_specs=[pl.BlockSpec(memory_space=pltpu.VMEM)] * 6,
        name="finish",
    )(*outs)
    return (*done[:4], done[4].reshape(64), done[5].reshape(64))


def solution(mesh):
    placed = (
        P("img", "seq", None),
        P("img", "seq", None),
        P("img", "seq", None),
        P("img", "seq", None),
        P("img", "seq"),
        P("img", "seq", None),
        P(),
        P(),
    )
    return jax.shard_map(
        functools.partial(local, mesh.shape["img"]),
        mesh=mesh,
        in_specs=placed,
        out_specs=(
            P("img", "seq", None),
            P("img", "seq", None),
            P("img", "seq", None),
            P("img", "seq", None),
            P(),
            P(),
        ),
        check_vma=False,
    )
```

```python
import functools

import jax
import jax.numpy as jnp
from jax import lax
from jax.experimental import pallas as pl
from jax.experimental.pallas import tpu as pltpu
from jax.sharding import PartitionSpec as P

BF = jnp.bfloat16
F32 = jnp.float32
EPSILON = 1e-06
NZ, NX = 8, 4
HEADS = ((0, 1, 0, 0), (0, 1, 64, 64), (2, 3, 0, 0), (2, 3, 64, 64), (4, 4, 0, 64))
Q_AT = {0: 0, 2: 1, 4: 2, 1: 3, 3: 4}
PARTS = ((0, 2), (2, 2), (4, 1))
PART_HEADS = ((0, 2), (2, 4), (4, 5))


def dot(a, b):
    return jnp.dot(a, b, preferred_element_type=F32)


def dot_t(a, b):
    return lax.dot_general(a, b, (((1,), (1,)), ((), ())), preferred_element_type=F32)


def dot_l(a, b):
    return lax.dot_general(a, b, (((0,), (0,)), ((), ())), preferred_element_type=F32)


def split(value):
    high = value.astype(BF)
    return high, (value - high.astype(F32)).astype(BF)


def kernel(
    ny,
    q_hbm,
    k_hbm,
    v_hbm,
    unmerge_in,
    g_hbm,
    q_gain,
    k_gain,
    att_out,
    gq_out,
    gk_out,
    gv_out,
    gain_out,
    q_unit,
    q_scale,
    k_unit,
    k_scale,
    kv_stage,
    qg_stage,
    kv,
    qg,
    qm,
    gm,
    q_t,
    g_t,
    es,
    acc,
    gq_acc,
    g_all,
    core_send,
    core_recv,
    up_send,
    up_recv,
    dn_send,
    dn_recv,
    out_stage,
    out_recv,
    cell_stage,
    cell_recv,
    gain_own,
    gain_x,
    gain_z,
    sem_xs,
    sem_xr,
    sem_us,
    sem_ur,
    sem_ds,
    sem_dr,
    sem_ps,
    sem_pr,
    sem_cs,
    sem_cr,
    sem_rus,
    sem_rur,
    sem_rds,
    sem_rdr,
    sem_gs,
    sem_gr,
    sem_fs,
    sem_fr,
    sem_in,
    q_in,
    k_in,
    v_in,
    g_in,
):
    img = lax.axis_index("img")
    seq = lax.axis_index("seq")
    core = seq % 2
    x = (seq // 2) % NX
    z = seq // (2 * NX)
    other = 1 - core

    def at(zz, xx, cc):
        return (img, (zz * NX + xx) * 2 + cc)

    sign = 1 - 2 * core
    onward = at((z + sign + NZ) % NZ, x, core)
    up = at((z + 1) % NZ, x, core)
    down = at((z + NZ - 1) % NZ, x, core)
    partner = at(z, x, other)
    x_peers = [at(z, (x + d) % NX, core) for d in range(1, NX)]
    z_peers = [at((z + d) % NZ, x, core) for d in range(1, NZ)]
    barrier = pltpu.get_barrier_semaphore()
    plane_peers = [partner] + [at(z, (x + d) % NX, c) for d in range(1, NX) for c in (core, other)]
    for e in range(1, ny):
        for d in range(NX):
            for c in (core, other):
                plane_peers.append(((img + e) % ny, (z * NX + (x + d) % NX) * 2 + c))
    greeted = plane_peers + z_peers
    for device in greeted:
        pl.semaphore_signal(barrier, inc=1, device_id=device, device_id_type=pl.DeviceIdType.MESH)

    def remote(src, dst, send_sem, recv_sem, device):
        return pltpu.make_async_remote_copy(
            src_ref=src,
            dst_ref=dst,
            send_sem=send_sem,
            recv_sem=recv_sem,
            device_id=device,
            device_id_type=pl.DeviceIdType.MESH,
        )

    loads = [
        pltpu.make_async_copy(src, dst, sem_in.at[i])
        for i, (src, dst) in enumerate(((k_hbm, k_in), (v_hbm, v_in), (q_hbm, q_in), (g_hbm, g_in)))
    ]
    loads[0].start()
    loads[1].start()
    lane = lax.broadcasted_iota(jnp.int32, (1, 128), 1)
    low = lane < 64
    head_sum = (
        (lax.broadcasted_iota(jnp.int32, (128, 128), 0) < 64)
        == (lax.broadcasted_iota(jnp.int32, (128, 128), 1) < 64)
    ).astype(F32).astype(BF)

    head_sum2 = jnp.concatenate([head_sum, head_sum], axis=0)

    def head_mean(value):
        return dot(jnp.concatenate(split(value), axis=1), head_sum2) * (1.0 / 64.0)

    gain_q = jnp.concatenate([q_gain[...], q_gain[...]], axis=1)
    gain_k = jnp.concatenate([k_gain[...], k_gain[...]], axis=1)
    cell = seq * 32 + lax.broadcasted_iota(jnp.int32, (32, 1), 0)
    member = (unmerge_in[...] == cell).astype(F32).astype(BF)

    def pick(first, second, which):
        if which == 0:
            return jnp.where(low, first, pltpu.roll(second, 64, 1)).astype(BF)
        return jnp.where(low, pltpu.roll(first, 64, 1), second).astype(BF)

    member2 = jnp.concatenate([member, member], axis=1)
    loads[0].wait()
    loads[2].start()
    loads[3].start()
    merged_k = []
    for two in range(5):
        normed = []
        for pair in (2 * two, 2 * two + 1):
            lanes = slice(pair * 128, pair * 128 + 128)
            raw = k_in[0, :, lanes].astype(F32)
            scale = lax.rsqrt(head_mean(raw * raw) + EPSILON)
            unit = raw * scale
            k_unit[:, lanes] = unit
            k_scale[:, lanes] = scale
            normed.append(unit * gain_k)
        rows = jnp.concatenate(split(jnp.concatenate(normed, axis=1)), axis=0)
        merged_k.append(dot(member2, rows) * 0.25)
    loads[1].wait()
    for two in range(5):
        merged_v = dot(member, v_in[0, :, two * 256 : two * 256 + 256]) * 0.25
        for i in range(2):
            one_k, one_v = merged_k[two][:, i * 128 : i * 128 + 128], merged_v[:, i * 128 : i * 128 + 128]
            if two < 4:
                kv_stage[two, 2 * i] = one_k.astype(BF)
                kv_stage[two, 2 * i + 1] = one_v.astype(BF)
            else:
                for which in range(2):
                    kv_stage[2 * i + which, 4] = pick(one_k, one_v, which)
    loads[2].wait()
    loads[3].wait()
    for pair in range(10):
        lanes = slice(pair * 128, pair * 128 + 128)
        raw = q_in[0, :, lanes].astype(F32)
        scale = lax.rsqrt(head_mean(raw * raw) + EPSILON)
        unit = raw * scale
        q_unit[:, lanes] = unit
        q_scale[:, lanes] = scale
        normed = (unit * gain_q).astype(BF).astype(F32) * 0.125
        if pair < 8:
            qg_stage[pair // 2, pair % 2] = normed.astype(BF)
        else:
            upstream = g_in[0, :, lanes].astype(F32)
            for which in range(2):
                qg_stage[(pair - 8) * 2 + which, 2] = pick(normed, upstream, which)
    for pair in range(8):
        qg_stage[pair // 2, 3 + pair % 2] = g_in[0, :, pair * 128 : pair * 128 + 128]
    def kv_x(d):
        return remote(
            kv_stage.at[(x + d) % NX],
            kv.at[:, z, core, pl.ds(pl.multiple_of(x * 32, 32), 32), :],
            sem_xs.at[0, d - 1],
            sem_xr.at[0, d - 1],
            x_peers[d - 1],
        )

    def qg_x(part, d):
        blocks = pl.ds(0, 3) if part == 0 else pl.ds(3, 2)
        return remote(
            qg_stage.at[(x + d) % NX, blocks],
            qg.at[x, blocks],
            sem_xs.at[1 + part, d - 1],
            sem_xr.at[1 + part, d - 1],
            x_peers[d - 1],
        )

    pl.semaphore_wait(barrier, len(greeted))

    for d in range(1, NX):
        kv_x(d).start()
    kv[:, z, core, pl.ds(pl.multiple_of(x * 32, 32), 32), :] = kv_stage[x]
    qg[x] = qg_stage[x]

    def z_slot(offset):
        return (z + offset + NZ) % NZ

    def blocks_of(part):
        return pl.ds(*PARTS[part])

    def far(s):
        return z_slot(-sign * s)

    def half(part):
        return core if part == 0 else other

    def ag_ring(s, part):
        ref = kv.at[:, far(s - 1), half(part)]
        return remote(ref, ref, sem_us.at[s - 1, part], sem_ur.at[s - 1, part], onward)

    def ag_partner(s, part):
        ref = kv.at[:, far(s), half(part)]
        return remote(ref, ref, sem_ps.at[s, part], sem_pr.at[s, part], partner)

    def piece(index, d):
        return kv.at[:, z, index, pl.ds(pl.multiple_of(((x + NX - d) % NX) * 32, 32), 32), :]

    def first_ring(part, d):
        ref = piece(half(part), d)
        return remote(ref, ref, sem_fs.at[part, d], sem_fr.at[part, d], onward)

    def first_partner(d):
        ref = piece(core, d)
        return remote(ref, ref, sem_fs.at[2, d], sem_fr.at[2, d], partner)

    def gather_hop(s, part):
        if s == 1:
            for d in range(NX):
                first_ring(part, d).wait_recv()
        else:
            ag_ring(s, part).wait_recv()
        if s < 3 or (s == 3 and part == 0):
            ag_ring(s + 1, part).start()
        ag_partner(s, part).start()

    for d in (0, 1, 3, 2):
        if d > 0:
            kv_x(d).wait_recv()
        first_ring(0, d).start()
        first_partner(d).start()
    for d in range(1, NX):
        qg_x(0, d).start()
    for d in (0, 1, 3, 2):
        first_partner(d).wait_recv()
        first_ring(1, d).start()

    def head_blocks(h):
        single = (h == 4).astype(jnp.int32)
        base = (h // 2) * 2
        q_block = base
        g_block = base + 1 - single
        q_lane = (h % 2) * 64
        g_lane = q_lane + 64 * single
        return q_block, g_block, pl.multiple_of(q_lane, 64), pl.multiple_of(g_lane, 64)

    def cell_rows(block, first, second):
        return jnp.concatenate(
            [kv[block, first].reshape(256, 128), kv[block, second].reshape(256, 128)], axis=0
        )

    def value_rows(block, g_lane, first, second):
        rows = cell_rows(block, first, second)
        mine = (lane < 64) == (g_lane < 64)
        return jnp.where(mine, rows, jnp.ones_like(rows))

    def forward(first, second, start, stop):
        def body(h, carry):
            q_block, g_block, q_lane, g_lane = head_blocks(h)
            scores = dot_t(qm[h], cell_rows(q_block, first, second))
            weights = jnp.exp(scores).astype(BF)
            es[h, first] = weights[:, :256]
            es[h, second] = weights[:, 256:]
            acc[h] += dot(weights, value_rows(g_block, g_lane, first, second))
            return carry

        lax.fori_loop(start, stop, body, 0)

    def forward_pair(s, start, stop):
        forward(far(s), far(1 - s), start, stop)

    def wait_partner(s):
        for part in range(2 if s < 4 else 1):
            ag_partner(s, part).wait_recv()

    acc[...] = jnp.zeros_like(acc)
    gq_acc[...] = jnp.zeros_like(gq_acc)
    gather_hop(1, 0)
    gather_hop(1, 1)
    for d in range(1, NX):
        qg_x(0, d).wait_recv()
    for h, (q_block, g_block, q_lane, g_lane) in enumerate(HEADS):
        rows = qg[:, Q_AT[q_block]].reshape(512, 128)
        qm[h] = jnp.where(low == (q_lane < 64), rows, jnp.zeros_like(rows))
        if h == 1:
            gather_hop(2, 0)
            for d in range(1, NX):
                qg_x(1, d).start()
    forward_pair(1, 0, 2)
    gather_hop(2, 1)
    forward_pair(1, 2, 5)
    gather_hop(3, 0)
    wait_partner(1)
    forward_pair(2, 0, 2)
    gather_hop(3, 1)
    forward_pair(2, 2, 5)
    for h, (q_block, g_block, q_lane, g_lane) in enumerate(HEADS):
        q_t[h] = jnp.transpose(qm[h].astype(F32))[q_lane : q_lane + 64].astype(BF)
    wait_partner(2)
    forward_pair(3, 0, 2)
    gather_hop(4, 0)
    forward_pair(3, 2, 5)
    wait_partner(3)
    wait_partner(4)
    def finish_head(h):
        q_block, g_block, q_lane, g_lane = HEADS[h]
        mine = low == (g_lane < 64)
        total = acc[h]
        inverse = pltpu.roll(1.0 / total, 64, 1)
        weighted = jnp.where(mine, total * inverse, 0.0).astype(BF)
        scaled = jnp.where(mine, qg[:, Q_AT[g_block]].reshape(512, 128).astype(F32) * inverse, 0.0).astype(BF)
        inner = jnp.sum(scaled.astype(F32) * weighted.astype(F32), axis=1, keepdims=True)
        high, rest = split(inner)
        spare = 64 - g_lane
        gm[h] = jnp.where(
            mine,
            scaled,
            jnp.where(lane == spare, -high, jnp.where(lane == spare + 1, -rest, jnp.zeros_like(scaled))),
        )
        g_t[h] = jnp.transpose(scaled.astype(F32))[g_lane : g_lane + 64].astype(BF)
        return weighted

    def finalize(part):
        if part == 0:
            pairs = (0,)
        else:
            pairs = (1,)
            out_stage[:, 4] = finish_head(4).reshape(4, 128, 128)
        for pair in pairs:
            first, second = finish_head(2 * pair), finish_head(2 * pair + 1)
            out_stage[:, pair] = jnp.where(low, first, second).reshape(4, 128, 128)

    def out_x(part, d):
        blocks = pl.ds(*((0, 2), (2, 1), (3, 2))[part])
        return remote(
            out_stage.at[(x + d) % NX, blocks],
            out_recv.at[x, blocks],
            sem_xs.at[3 + part, d - 1],
            sem_xr.at[3 + part, d - 1],
            x_peers[d - 1],
        )

    def backward(step, first, second, start, stop):
        def body(h, carry):
            q_block, g_block, q_lane, g_lane = head_blocks(h)
            keys = cell_rows(q_block, first, second)
            weights = jnp.concatenate([es[h, first], es[h, second]], axis=1)
            change = dot_t(gm[h], value_rows(g_block, g_lane, first, second))
            grads = (change * weights.astype(F32)).astype(BF)
            gq_acc[h] += dot(grads, keys)
            key_part = dot(q_t[h], grads)
            value_part = dot(g_t[h], weights)
            for i in range(2):
                for c in range(2):
                    cols = slice(i * 256 + c * 128, i * 256 + c * 128 + 128)
                    g_all[step, i, c, q_block, pl.ds(q_lane, 64), :] = key_part[:, cols]
                    g_all[step, i, c, g_block, pl.ds(g_lane, 64), :] = value_part[:, cols]
            return carry

        lax.fori_loop(start, stop, body, 0)

    def core_copy(step, part):
        blocks = blocks_of(part)
        return remote(
            core_send.at[step, :, blocks],
            core_recv.at[step, :, blocks],
            sem_cs.at[step, part],
            sem_cr.at[step, part],
            partner,
        )

    def rs_up(hop, part):
        blocks = blocks_of(part)
        return remote(
            up_send.at[hop, blocks], up_recv.at[hop, blocks], sem_rus.at[hop, part], sem_rur.at[hop, part], up
        )

    def rs_down(hop, part):
        blocks = blocks_of(part)
        return remote(
            dn_send.at[hop, blocks], dn_recv.at[hop, blocks], sem_rds.at[hop, part], sem_rdr.at[hop, part], down
        )

    def chip_sum(step, i, part):
        blocks = blocks_of(part)
        return g_all[step, i, core, blocks] + core_recv[step, i, blocks].astype(F32)

    def send_up(hop, step, i, part):
        value = chip_sum(step, i, part)
        blocks = blocks_of(part)
        if hop > 0 and not (hop == 1 and part > 0):
            rs_up(hop - 1, part).wait_recv()
            value = value + up_recv[hop - 1, blocks].astype(F32)
        up_send[hop, blocks] = value.astype(BF)
        rs_up(hop, part).start()

    def send_down(hop, step, i, part):
        value = chip_sum(step, i, part)
        blocks = blocks_of(part)
        if hop > 0 and not (hop == 1 and part == 0):
            rs_down(hop - 1, part).wait_recv()
            value = value + dn_recv[hop - 1, blocks].astype(F32)
        dn_send[hop, blocks] = value.astype(BF)
        rs_down(hop, part).start()

    def reduce_half(step, part):
        core_copy(step, part).wait_recv()
        if step == 0 and part == 0:
            send_up(0, 0, 0, 0)
        elif step == 0:
            send_down(0, 0, 0, part)
            send_up(1, 0, 1, part)
        elif step == 1 and part == 0:
            send_down(1, 1, 0, 0)
            send_up(1, 0, 1, 0)
        elif step < 3:
            if step == 2 and part == 0:
                send_up(2, 1, 1, 0)
            send_down(step, step, 0, part)
            if part > 0:
                send_up(step + 1, step, 1, part)
        else:
            if part == 0:
                send_up(3, 2, 1, 0)
            send_down(3, 3, 0, part)

    def backward_half(step, part):
        first = z_slot((4, -3, -2, -1)[step])
        second = z_slot((3, 2, 1, 0)[step])
        backward(step, first, second, *PART_HEADS[part])
        blocks = blocks_of(part)
        core_send[step, :, blocks] = g_all[step, :, other, blocks].astype(BF)
        core_copy(step, part).start()

    forward_pair(4, 0, 2)
    for d in range(1, NX):
        qg_x(1, d).wait_recv()
    finalize(0)
    backward_half(0, 0)
    forward_pair(4, 2, 5)
    finalize(1)
    for d in range(1, NX):
        out_x(0, d).start()
    reduce_half(0, 0)
    backward_half(0, 1)
    backward_half(0, 2)
    backward_half(1, 0)
    reduce_half(0, 1)
    reduce_half(0, 2)
    backward_half(1, 1)
    backward_half(1, 2)
    reduce_half(1, 0)
    backward_half(2, 0)
    reduce_half(1, 1)
    reduce_half(1, 2)
    backward_half(2, 1)
    backward_half(2, 2)
    reduce_half(2, 0)
    backward_half(3, 0)
    out_stage[:, 2] = jnp.where(low, gq_acc[0], gq_acc[1]).astype(BF).reshape(4, 128, 128)
    for d in range(1, NX):
        out_x(1, d).start()
    reduce_half(2, 1)
    reduce_half(2, 2)
    backward_half(3, 1)
    backward_half(3, 2)

    def gain_copies(stage):
        base, buffer, mine, peers = gain_stages[stage]
        return [
            remote(gain_own.at[stage], buffer.at[mine], sem_gs.at[base + i], sem_gr.at[base + i], device)
            for i, device in enumerate(peers)
        ]

    def gain_send(stage, value):
        base, buffer, mine, peers = gain_stages[stage]
        gain_own[stage] = value
        for copy in gain_copies(stage):
            copy.start()
        buffer[mine] = value

    def gain_sum(stage):
        base, buffer, mine, peers = gain_stages[stage]
        for copy in gain_copies(stage):
            copy.wait_recv()
        result = buffer[0]
        for i in range(1, len(peers) + 1):
            result = result + buffer[i]
        return result

    gain_stages = (
        (0, gain_x, (img * NX + x) * 2 + core, plane_peers),
        (len(plane_peers), gain_z, z, z_peers),
    )
    tile = jnp.zeros((8, 128), F32)
    for h in range(5):
        tile = tile + jnp.sum((qm[h].astype(F32) * gq_acc[h]).reshape(64, 8, 128), axis=0)
    gain_send(0, jnp.sum(tile, axis=0, keepdims=True))
    reduce_half(3, 0)

    out_stage[:, 3] = jnp.where(low, gq_acc[2], gq_acc[3]).astype(BF).reshape(4, 128, 128)
    out_stage[:, 4] = (
        jnp.where(low, gq_acc[4], out_stage[:, 4].reshape(512, 128).astype(F32))
        .astype(BF)
        .reshape(4, 128, 128)
    )
    for d in range(1, NX):
        out_x(2, d).start()
    out_recv[x] = out_stage[x]
    reduce_half(3, 1)
    reduce_half(3, 2)

    def join(first, second, which):
        if which == 0:
            return jnp.where(low, first, pltpu.roll(second, 64, 1))
        return jnp.where(low, pltpu.roll(first, 64, 1), second)

    def cell_x(part, d):
        blocks = blocks_of(part)
        rows = pl.ds(pl.multiple_of(((x + d) % NX) * 32, 32), 32)
        return remote(
            cell_stage.at[blocks, rows, :],
            cell_recv.at[x, blocks],
            sem_xs.at[6 + part, d - 1],
            sem_xr.at[6 + part, d - 1],
            x_peers[d - 1],
        )

    def final_sum():
        for part in range(3):
            rs_up(3, part).wait_recv()
            rs_down(3, part).wait_recv()
            first, count = PARTS[part]
            for b in range(first, first + count):
                total = (
                    g_all[3, 1, core, b]
                    + core_recv[3, 1, b].astype(F32)
                    + up_recv[3, b].astype(F32)
                    + dn_recv[3, b].astype(F32)
                )
                cell_stage[b] = jnp.transpose(total).astype(BF)
            for d in range(1, NX):
                cell_x(part, d).start()

    for d in range(1, NX):
        out_x(0, d).wait_recv()
    for pair in range(8):
        att_out[0, :, pair * 128 : pair * 128 + 128] = out_recv[pair // 2, pair % 2]
    final_sum()
    cell_recv[x] = cell_stage[:, pl.ds(pl.multiple_of(x * 32, 32), 32), :]
    gain_send(1, gain_sum(0))

    for part in (1, 2):
        for d in range(1, NX):
            out_x(part, d).wait_recv()
    for pair in range(10):
        lanes = slice(pair * 128, pair * 128 + 128)
        if pair < 8:
            grad = out_recv[pair // 2, 2 + pair % 2].astype(F32)
        else:
            one = out_recv[(pair - 8) * 2, 4].astype(F32)
            two = out_recv[(pair - 8) * 2 + 1, 4].astype(F32)
            att_out[0, :, lanes] = join(one, two, 1).astype(BF)
            grad = join(one, two, 0)
        grad = grad * 0.125 * gain_q
        unit = q_unit[:, lanes]
        inner = head_mean(grad * unit)
        gq_out[0, :, lanes] = (q_scale[:, lanes] * (grad - unit * inner)).astype(BF)

    for part in range(3):
        for d in range(1, NX):
            cell_x(part, d).wait_recv()
    for pair in range(10):
        lanes = slice(pair * 128, pair * 128 + 128)
        if pair < 8:
            cell_k = cell_recv[pair // 2, (pair % 2) * 2]
            cell_v = cell_recv[pair // 2, (pair % 2) * 2 + 1]
        else:
            one = cell_recv[(pair - 8) * 2, 4].astype(F32)
            two = cell_recv[(pair - 8) * 2 + 1, 4].astype(F32)
            cell_k = join(one, two, 0).astype(BF)
            cell_v = join(one, two, 1).astype(BF)
        gv_out[0, :, lanes] = (dot_l(member, cell_v) * 0.25).astype(BF)
        grad = dot_l(member, cell_k) * 0.25 * gain_k
        unit = k_unit[:, lanes]
        inner = head_mean(grad * unit)
        gk_out[0, :, lanes] = (k_scale[:, lanes] * (grad - unit * inner)).astype(BF)

    row = gain_sum(1)
    row = row + pltpu.roll(row, 64, 1)
    gain_out[...] = jnp.broadcast_to(row / jnp.where(low, gain_q, gain_k), (8, 128))

    for d in range(1, NX):
        kv_x(d).wait_send()
        for part in range(2):
            qg_x(part, d).wait_send()
        for part in range(3):
            out_x(part, d).wait_send()
        for part in range(3):
            cell_x(part, d).wait_send()
    for d in range(NX):
        first_partner(d).wait_send()
        for part in range(2):
            first_ring(part, d).wait_send()
    for s in range(1, 5):
        for part in range(2):
            if s < 4 or part == 0:
                if s > 1:
                    ag_ring(s, part).wait_send()
                ag_partner(s, part).wait_send()
    for step in range(4):
        for part in range(3):
            core_copy(step, part).wait_send()
            if step > 0 or part == 0:
                rs_up(step, part).wait_send()
            if step > 0 or part > 0:
                rs_down(step, part).wait_send()
    for stage in range(2):
        for copy in gain_copies(stage):
            copy.wait_send()


def finish(att, gq, gk, gv, gain, att_out, gq_out, gk_out, gv_out, q_gain_out, k_gain_out):
    att_out[...] = att[...]
    gq_out[...] = gq[...]
    gk_out[...] = gk[...]
    gv_out[...] = gv[...]
    q_gain_out[...] = gain[0:1, :64]
    k_gain_out[...] = pltpu.roll(gain[...], 64, 1)[0:1, :64]


def local(ny, query_proj, key_proj, value_proj, merge_cells, unmerge, grad_out, query_gain, key_gain):
    vmem = pltpu.VMEM
    dma = pltpu.SemaphoreType.DMA
    block = (5, 128, 128)
    outs = pl.pallas_call(
        functools.partial(kernel, ny),
        out_shape=[jax.ShapeDtypeStruct((1, 128, 1280), BF)] * 4
        + [jax.ShapeDtypeStruct((8, 128), F32)],
        in_specs=[pl.BlockSpec(memory_space=pl.ANY)] * 3
        + [pl.BlockSpec(memory_space=pltpu.VMEM), pl.BlockSpec(memory_space=pl.ANY)]
        + [pl.BlockSpec(memory_space=pltpu.VMEM)] * 2,
        out_specs=[pl.BlockSpec(memory_space=pltpu.VMEM)] * 5,
        scratch_shapes=[
            vmem((128, 1280), F32),
            vmem((128, 1280), F32),
            vmem((128, 1280), F32),
            vmem((128, 1280), F32),
            vmem((4, 5, 32, 128), BF),
            vmem((4,) + block, BF),
            vmem((5, 8, 2, 128, 128), BF),
            vmem((4,) + block, BF),
            vmem((5, 512, 128), BF),
            vmem((5, 512, 128), BF),
            vmem((5, 64, 512), BF),
            vmem((5, 64, 512), BF),
            vmem((5, 8, 512, 256), BF),
            vmem((5, 512, 128), F32),
            vmem((5, 512, 128), F32),
            vmem((4, 2, 2) + block, F32),
            vmem((4, 2) + block, BF),
            vmem((4, 2) + block, BF),
            vmem((4,) + block, BF),
            vmem((4,) + block, BF),
            vmem((4,) + block, BF),
            vmem((4,) + block, BF),
            vmem((4,) + block, BF),
            vmem((4,) + block, BF),
            vmem(block, BF),
            vmem((4, 5, 32, 128), BF),
            vmem((2, 1, 128), F32),
            vmem((2 * NX * ny, 1, 128), F32),
            vmem((NZ, 1, 128), F32),
            dma((9, 3)),
            dma((9, 3)),
            dma((4, 3)),
            dma((4, 3)),
            dma((4, 3)),
            dma((4, 3)),
            dma((8, 2)),
            dma((8, 2)),
            dma((4, 3)),
            dma((4, 3)),
            dma((4, 3)),
            dma((4, 3)),
            dma((4, 3)),
            dma((4, 3)),
            dma((2 * NX * ny - 1 + NZ - 1,)),
            dma((2 * NX * ny - 1 + NZ - 1,)),
            dma((3, 4)),
            dma((3, 4)),
            dma((4,)),
            vmem((1, 128, 1280), BF),
            vmem((1, 128, 1280), BF),
            vmem((1, 128, 1280), BF),
            vmem((1, 128, 1280), BF),
        ],
        compiler_params=pltpu.CompilerParams(
            collective_id=0, has_side_effects=True, vmem_limit_bytes=60 * 1024 * 1024
        ),
        name="attention_block",
    )(
        query_proj,
        key_proj,
        value_proj,
        unmerge,
        grad_out,
        query_gain.reshape(1, 64),
        key_gain.reshape(1, 64),
    )
    done = pl.pallas_call(
        finish,
        out_shape=[jax.ShapeDtypeStruct((1, 128, 1280), BF)] * 4 + [jax.ShapeDtypeStruct((1, 64), F32)] * 2,
        in_specs=[pl.BlockSpec(memory_space=pltpu.VMEM)] * 5,
        out_specs=[pl.BlockSpec(memory_space=pltpu.VMEM)] * 6,
        name="finish",
    )(*outs)
    return (*done[:4], done[4].reshape(64), done[5].reshape(64))


def solution(mesh):
    placed = (
        P("img", "seq", None),
        P("img", "seq", None),
        P("img", "seq", None),
        P("img", "seq", None),
        P("img", "seq"),
        P("img", "seq", None),
        P(),
        P(),
    )
    return jax.shard_map(
        functools.partial(local, mesh.shape["img"]),
        mesh=mesh,
        in_specs=placed,
        out_specs=(
            P("img", "seq", None),
            P("img", "seq", None),
            P("img", "seq", None),
            P("img", "seq", None),
            P(),
            P(),
        ),
        check_vma=False,
    )
```
